32 devices in a mesh: chan: 4 (over y, x), facet: 8 (over z, core).
Axes of the slice: x: 2, y: 2, z: 4, core: 2. Of those that a mesh axis runs over, the one named last changes fastest.
Arguments:
- dirty_image: float32 [64, 256, 256], P('chan', 'facet'), may hold values from -6 to 6
- image_start: float32 [64, 256, 256], P('chan', 'facet'), may hold values from 0 to 1
- dual_start: float32 [64, 2, 256, 256], P('chan', None, 'facet'), may hold values from -1.8 to 1.8
- psf_rows: float32 [64, 17], P('chan'), may hold values from -1 to 1, as said below
- psf_cols: float32 [64, 17], P('chan'), may hold values from -1 to 1, as said below
- wavelet_taps: float32 [2, 17], replicated, may hold values from -1 to 1, as said below
- channel_flags: int32 [64], P('chan'), may hold values 0 or 1
Outputs:
- image_final: float32 [64, 256, 256], P('chan', 'facet')
- dual_final: float32 [64, 2, 256, 256], P('chan', None, 'facet')
The draws below stay inside these ranges and needn't reach their ends.
Inputs may be any that keep to these rules, and one draw needn't show every extreme that they name: `psf_rows`: each channel's taps have absolute values summing to 1. `psf_cols`: each channel's taps have absolute values summing to 1. `wavelet_taps`: each filter sums to zero and its absolute values sum to 1.
All inputs are finite; a program needn't handle non-finite values. No bound on the sum of `channel_flags` on one device may be relied on, other than what follows from the above.
Results may differ from the reference program's by a relative error of at most 0.0001.
Values sent between devices are 32-bit elements; how exact they have to be, the bound alone decides.
No kernel may reach another device: no remote copies, remote signals or barrier semaphores. Data moves between devices by JAX's collectives and lax.ppermute only.
A program may use at most 128 MiB of HBM per device.

```python
import jax
import jax.numpy as jnp
from jax import lax

COLS = 256
PSF_HALF = 8
WAV_HALF = 8
OUTER = 2
INNER = 3
CHANS = 64
NROWS = 256


def psf_table(key):
    shape = (CHANS, 2 * PSF_HALF + 1)
    values = jax.random.normal(key, shape, jnp.float32)
    return values / jnp.sum(jnp.abs(values), axis=1, keepdims=True)


def draw_psf_rows(key, part):
    return psf_table(jax.random.fold_in(key, 101))


def draw_psf_cols(key, part):
    return psf_table(jax.random.fold_in(key, 202))


def draw_wavelet_taps(key, part):
    shape = (2, 2 * WAV_HALF + 1)
    inner_key = jax.random.fold_in(key, 303)
    values = jax.random.normal(inner_key, shape, jnp.float32)
    values = values - jnp.mean(values, axis=1, keepdims=True)
    return values / jnp.sum(jnp.abs(values), axis=1, keepdims=True)


def touch_ends(entries, own_key, least, largest):
    longest = entries.shape.index(max(entries.shape))
    spots = []
    for shift in (0, 1):
        where = [jax.random.randint(jax.random.fold_in(own_key, axis), (), 0, length) for axis, length in enumerate(entries.shape)]
        where[longest] = (where[longest] + shift) % entries.shape[longest]
        spots.append(tuple(where))
    return entries.at[spots[0]].set(least).at[spots[1]].set(largest)


def block_levels(rng, dims, pieces, low, high):
    def one(axis_at, shards_of):
        draws = jax.random.uniform(jax.random.fold_in(jax.random.fold_in(rng, 6), axis_at), (shards_of,), jnp.float32, low / len(pieces), high / len(pieces))
        return jnp.repeat(jnp.exp(draws), dims[axis_at] // shards_of).reshape((-1,) + (1,) * (len(dims) - axis_at - 1))

    gain = one(*pieces[0])
    for cut in pieces[1:]:
        gain = gain * one(*cut)
    return gain


def centred(key, shape, deviation, most, split=(), kind=jnp.bfloat16):
    drawn = deviation * jax.random.normal(key, shape, jnp.float32)
    if split:
        drawn = drawn * block_levels(key, shape, split, -0.22, 0.18)
    return jnp.clip(drawn, -most, most).astype(kind)


def setup_inputs(seed: int = 0) -> dict:
    streams_of = jax.random.split(jax.random.key(seed), 8)
    return {
        "dirty_image": centred(streams_of[0], (CHANS, NROWS, COLS), 1.0, 6.0, ((0, 4), (1, 8)), jnp.float32),
        "image_start": jnp.clip(1.0 * jax.random.uniform(streams_of[1], (CHANS, NROWS, COLS), jnp.float32) ** block_levels(streams_of[1], (CHANS, NROWS, COLS), ((0, 4), (1, 8)), -0.2, 0.2), 0.0, 1.0),
        "dual_start": centred(streams_of[2], (CHANS, 2, NROWS, COLS), 0.3, 1.8, ((0, 4), (2, 8)), jnp.float32),
        "psf_rows": draw_psf_rows(jax.random.fold_in(streams_of[7], 71), 0),
        "psf_cols": draw_psf_cols(jax.random.fold_in(streams_of[7], 71), 0),
        "wavelet_taps": draw_wavelet_taps(jax.random.fold_in(streams_of[7], 71), 0),
        "channel_flags": touch_ends((jax.random.randint(streams_of[6], (CHANS,), 0, 8) < 7).astype(jnp.int32), jax.random.fold_in(streams_of[6], 1), 0, 1),
    }


STEP_PRIMAL = 0.9
STEP_DUAL = 0.2
RADIUS_SCALE = 0.06
WEIGHT_OFFSET = 1.0

def rows_forward(values, filter_taps, half_width):
    height = values.shape[1]
    padded = jnp.pad(values, ((0, 0), (half_width, half_width), (0, 0)))
    summed = jnp.zeros_like(values)
    for offset in range(2 * half_width + 1):
        summed = summed + filter_taps[:, offset][:, None, None] * padded[:, offset:offset + height]
    return summed

def rows_adjoint(values, filter_taps, half_width):
    height = values.shape[1]
    padded = jnp.pad(values, ((0, 0), (half_width, half_width), (0, 0)))
    summed = jnp.zeros_like(values)
    for offset in range(2 * half_width + 1):
        start = 2 * half_width - offset
        summed = summed + filter_taps[:, offset][:, None, None] * padded[:, start:start + height]
    return summed

def cols_forward(values, filter_taps, half_width):
    columns = values.shape[2]
    padded = jnp.pad(values, ((0, 0), (0, 0), (half_width, half_width)))
    summed = jnp.zeros_like(values)
    for offset in range(2 * half_width + 1):
        summed = summed + filter_taps[:, offset][:, None, None] * padded[:, :, offset:offset + columns]
    return summed

def cols_adjoint(values, filter_taps, half_width):
    columns = values.shape[2]
    padded = jnp.pad(values, ((0, 0), (0, 0), (half_width, half_width)))
    summed = jnp.zeros_like(values)
    for offset in range(2 * half_width + 1):
        start = 2 * half_width - offset
        summed = summed + filter_taps[:, offset][:, None, None] * padded[:, :, start:start + columns]
    return summed

def analysis(values, wavelet_taps):
    return jnp.stack([rows_forward(values, wavelet_taps[0:1], WAV_HALF), cols_forward(values, wavelet_taps[1:2], WAV_HALF)], axis=1)

def synthesis(dual_field, wavelet_taps):
    return rows_adjoint(dual_field[:, 0], wavelet_taps[0:1], WAV_HALF) + cols_adjoint(dual_field[:, 1], wavelet_taps[1:2], WAV_HALF)

def reference(dirty_image, image_start, dual_start, psf_rows, psf_cols, wavelet_taps, channel_flags):
    weight_data = channel_flags.astype(jnp.float32)[:, None, None]
    estimate = image_start
    dual_field = dual_start
    for outer_step in range(OUTER):
        coeffs = analysis(estimate, wavelet_taps)
        weights = 1.0 / (jnp.sqrt(lax.optimization_barrier(jnp.sum(coeffs * coeffs, axis=0))) + WEIGHT_OFFSET)
        radius = RADIUS_SCALE * CHANS * weights
        for inner_step in range(INNER):
            blurred = cols_forward(rows_forward(estimate, psf_rows, PSF_HALF), psf_cols, PSF_HALF)
            residual = weight_data * (blurred - dirty_image)
            gradient = rows_adjoint(cols_adjoint(residual, psf_cols, PSF_HALF), psf_rows, PSF_HALF)
            updated = jnp.maximum(estimate - STEP_PRIMAL * (gradient + synthesis(dual_field, wavelet_taps)), 0.0)
            dual_moved = dual_field + STEP_DUAL * analysis(2.0 * updated - estimate, wavelet_taps)
            length = jnp.sqrt(lax.optimization_barrier(jnp.sum(dual_moved * dual_moved, axis=0)))
            dual_field = dual_moved * (radius / jnp.maximum(length, radius))
            estimate = updated
    return (estimate, dual_field)
```

```python
import functools

import jax
import jax.numpy as jnp
from jax import lax
from jax.experimental import pallas as pl
from jax.experimental.pallas import tpu as pltpu
from jax.sharding import PartitionSpec as P

PSF_HALF = 8
WAV_HALF = 8
OUTER = 2
INNER = 3

STEP_PRIMAL = 0.9
STEP_DUAL = 0.2
RADIUS_SCALE = 0.06
WEIGHT_OFFSET = 1.0

F32 = jnp.float32
BF16 = jnp.bfloat16
VMEM_LIMIT = 24 * 1024 * 1024
PARAMS = pltpu.CompilerParams(vmem_limit_bytes=VMEM_LIMIT)


def split(values):
    head = values.astype(BF16)
    return head, (values - head.astype(F32)).astype(BF16)


def times_columns(values, head, rest):
    rows = values.shape[0]
    first, second = split(values)
    both = jnp.dot(jnp.concatenate([first, second], axis=0), head, preferred_element_type=F32)
    return both[:rows] + both[rows:] + jnp.dot(first, rest, preferred_element_type=F32)


def stacked(values):
    first, second = split(values)
    return jnp.concatenate([first, second, first], axis=0)


def split_outside(values):
    head = lax.reduce_precision(values, 8, 7)
    return head.astype(BF16), (values - head).astype(BF16)


def wide(matrix):
    first, second = split_outside(matrix)
    return jnp.concatenate([first, first, second], axis=-1)


VM = pl.BlockSpec(memory_space=pltpu.VMEM)
SM = pl.BlockSpec(memory_space=pltpu.SMEM)


def call(kernel, ins, outs, name, scalars=0):
    return pl.pallas_call(
        kernel,
        out_shape=[jax.ShapeDtypeStruct(shape, F32) for shape in outs],
        in_specs=[SM] * scalars + [VM] * (len(ins) - scalars),
        out_specs=[VM] * len(outs),
        compiler_params=PARAMS,
        name=name,
    )(*ins)


def rows_kernel(first, odd_ref, own_ref, near_ref, far_ref, mats_ref, *rest):
    if first:
        band_ref, part_ref = rest
    else:
        dual_ref, old_ref, sum1_ref, band_ref, part_ref, moved_ref, sums_ref = rest
    chans, height, width = own_ref.shape
    reach = dual_height = band_ref.shape[1]
    odd = odd_ref[0] == 1

    def body(c, total):
        near, far = near_ref[c], far_ref[c]
        before = jnp.where(odd, near, far)
        after = jnp.where(odd, far, near)
        extended = jnp.concatenate([before, own_ref[c], after], axis=0)
        product = jnp.dot(mats_ref[c], stacked(extended), preferred_element_type=F32)
        band, part = product[:reach], product[reach:]
        band_ref[c] = band
        part_ref[c] = part
        if first:
            return total
        moved = dual_ref[c] + STEP_DUAL * (2.0 * band - old_ref[c])
        moved_ref[c] = moved
        return total + moved * moved

    total = lax.fori_loop(0, chans, body, jnp.zeros((dual_height, width), F32), unroll=2)
    if not first:
        sums_ref[:dual_height] = total
        sums_ref[dual_height:] = sum1_ref[...]


def squares_kernel(first_ref, second_ref, out_ref):
    low = first_ref.shape[1]
    out_ref[:low] = jnp.sum(first_ref[...] * first_ref[...], axis=0)
    out_ref[low:] = jnp.sum(second_ref[...] * second_ref[...], axis=0)


def columns_kernel(own_ref, head_ref, rest_ref, dual_ref, old_ref, band_ref, moved_ref, sum_ref):
    chans, height, width = own_ref.shape
    group = 8
    total = jnp.zeros((height, width), F32)
    for c in range(0, chans, group):
        n = min(group, chans - c)
        band = times_columns(
            own_ref[c : c + n].reshape(n * height, width), head_ref[...], rest_ref[...]
        ).reshape(n, height, width)
        band_ref[c : c + n] = band
        moved = dual_ref[c : c + n] + STEP_DUAL * (2.0 * band - old_ref[c : c + n])
        moved_ref[c : c + n] = moved
        total = total + jnp.sum(moved * moved, axis=0)
    sum_ref[...] = total


def analysis_columns_kernel(own_ref, head_ref, rest_ref, band_ref):
    chans, height, width = own_ref.shape
    group = 8
    for c in range(0, chans, group):
        n = min(group, chans - c)
        band_ref[c : c + n] = times_columns(
            own_ref[c : c + n].reshape(n * height, width), head_ref[...], rest_ref[...]
        ).reshape(n, height, width)


def gradient_kernel(part_ref, head_ref, rest_ref, data_ref, grad_ref):
    chans = part_ref.shape[0]

    def body(c, carry):
        grad_ref[c] = times_columns(part_ref[c], head_ref[c], rest_ref[c]) - data_ref[c]
        return carry

    lax.fori_loop(0, chans, body, 0, unroll=2)


def scaled(sums_refs, radius):
    total = sums_refs[0][...]
    for ref in sums_refs[1:]:
        total = total + ref[...]
    length = jnp.sqrt(total)
    return radius / jnp.maximum(length, radius)


def update_kernel(n_sums, odd_ref, *refs):
    sums_refs, refs = refs[:n_sums], refs[n_sums:]
    if n_sums:
        radius_ref, refs = refs[0], refs[1:]
    (
        moved0_ref, moved1_ref, own_ref, grad_ref, rows_ref, head_ref, rest_ref,
        new_ref, near_ref, far_ref, *duals,
    ) = refs
    chans, height, width = own_ref.shape
    reach = moved0_ref.shape[1]
    send = near_ref.shape[1]
    odd = odd_ref[0] == 1
    if n_sums:
        dual0_ref, dual1_ref = duals
        scale = scaled(sums_refs, radius_ref[...])
        scale0, scale1 = scale[:reach], scale[reach:]
    group = 4
    for c0 in range(0, chans, group):
        n = min(group, chans - c0)
        dual1 = moved1_ref[c0 : c0 + n]
        if n_sums:
            dual1 = dual1 * scale1[None]
            dual1_ref[c0 : c0 + n] = dual1
        across = times_columns(dual1.reshape(n * height, width), head_ref[...], rest_ref[...])
        for c in range(c0, c0 + n):
            dual0 = moved0_ref[c]
            if n_sums:
                dual0 = dual0 * scale0
                dual0_ref[c] = dual0
            down = jnp.dot(rows_ref[...], stacked(dual0), preferred_element_type=F32)
            at = (c - c0) * height
            step = grad_ref[c] + (down + across[at : at + height])
            new = jnp.maximum(own_ref[c] - STEP_PRIMAL * step, 0.0)
            new_ref[c] = new
            top, bottom = new[:send], new[height - send :]
            near_ref[c] = jnp.where(odd, top, bottom)
            far_ref[c] = jnp.where(odd, bottom, top)


def final_kernel(n_sums, *refs):
    sums_refs, refs = refs[:n_sums], refs[n_sums:]
    radius_ref, moved0_ref, moved1_ref, dual_ref = refs
    height = moved1_ref.shape[1]
    reach = moved0_ref.shape[1]
    pad = (reach - height) // 2
    scale = scaled(sums_refs, radius_ref[...])
    scale0, scale1 = scale[pad : pad + height], scale[reach:]
    for c in range(moved1_ref.shape[0]):
        dual_ref[c, 0] = moved0_ref[c, pad : pad + height] * scale0
        dual_ref[c, 1] = moved1_ref[c] * scale1


def exchange(near, far):
    n = lax.axis_size("facet")
    pair = [(i, i ^ 1) for i in range(n)]
    cross = [(i, ((i + 1) ^ 1) - 1) for i in range(n) if 0 <= ((i + 1) ^ 1) - 1 < n]
    return lax.ppermute(near, "facet", pair), lax.ppermute(far, "facet", cross)


def gathered(sums):
    n = lax.axis_size("chan")
    if n & (n - 1):
        return [lax.psum(sums, "chan")]
    low = 1
    terms = [sums]
    while low < n:
        radix = min(4, n // low)
        total = terms[0]
        for term in terms[1:]:
            total = total + term
        terms = [total] + [
            lax.ppermute(total, "chan", [(i, i ^ (k * low)) for i in range(n)])
            for k in range(1, radix)
        ]
        low *= radix
    return terms


def toeplitz(taps, rows, cols, shift):
    offset = jnp.arange(cols)[None, :] - jnp.arange(rows)[:, None] + shift
    total = jnp.zeros(taps.shape[:-1] + (rows, cols), F32)
    for k in range(taps.shape[-1]):
        total = total + jnp.where(offset == k, taps[..., k][..., None, None], 0.0)
    return total


HIGH = lax.Precision.HIGHEST


def on_device(
    dirty_image, image_start, dual_start, psf_rows, psf_cols, wavelet_taps, channel_flags
):
    chans, height, width = image_start.shape
    facet, facets = lax.axis_index("facet"), lax.axis_size("facet")
    total_chans = chans * lax.axis_size("chan")
    hp, hw = PSF_HALF, WAV_HALF
    near_by = hw
    reach = height + 2 * near_by
    send = 2 * near_by
    odd = (facet % 2).astype(jnp.int32)
    odd_arg = odd[None]
    is_odd = odd == 1
    used = channel_flags.astype(F32)[:, None, None]

    at = jnp.arange(reach)
    inside = jnp.where(at < near_by, facet > 0, jnp.where(at >= near_by + height, facet < facets - 1, True))
    inside = inside.astype(F32)

    tall = height + 2 * send
    psf_r = toeplitz(psf_rows, reach, tall, 0)
    psf_r_adj = toeplitz(psf_rows[:, ::-1], height, reach, 0)
    normal = jnp.einsum("coa,a,cab->cob", psf_r_adj, inside, psf_r, precision=HIGH) * used
    wav_r = toeplitz(wavelet_taps[0], reach, tall, 0) * inside[:, None]
    wav_r_adj = toeplitz(wavelet_taps[0, ::-1], height, reach, 0)
    mats = wide(jnp.concatenate([jnp.broadcast_to(wav_r[None], (chans,) + wav_r.shape), normal], axis=1))
    wav_rows = wide(wav_r_adj)

    psf_c = toeplitz(psf_cols[:, ::-1], width, width, hp)
    around = jnp.einsum("cij,ckj->cik", psf_c, psf_c, precision=HIGH)
    around_head, around_rest = split_outside(around)
    wav_c = toeplitz(wavelet_taps[1, ::-1], width, width, hw)
    wav_head, wav_rest = split_outside(wav_c)
    wav_head_t, wav_rest_t = wav_head.T, wav_rest.T

    def edges(rows, of):
        return of[:, :rows], of[:, height - rows :]

    tops, bottoms = zip(
        edges(send, image_start), edges(near_by, dual_start[:, 0]), edges(near_by, dirty_image)
    )
    top, bottom = jnp.concatenate(tops, axis=1), jnp.concatenate(bottoms, axis=1)
    near, far = exchange(jnp.where(is_odd, top, bottom), jnp.where(is_odd, bottom, top))
    before, after = jnp.where(is_odd, near, far), jnp.where(is_odd, far, near)

    def extended(own, start, rows):
        return jnp.concatenate(
            [before[:, start : start + rows], own, after[:, start : start + rows]], axis=1
        )

    moved0 = extended(dual_start[:, 0], send, near_by)
    moved1 = dual_start[:, 1]
    data = extended(dirty_image, send + near_by, near_by)
    data = jnp.einsum("coa,caj,ckj->cok", psf_r_adj, data, psf_c, precision=HIGH) * used

    own_shape = (chans, height, width)
    tall_shape = (chans, reach, width)
    part_shape = own_shape
    sum_shape = (reach + height, width)
    send_shape = (chans, send, width)

    def gradient(part):
        return call(gradient_kernel, (part, around_head, around_rest, data), (own_shape,), "gradient")[0]

    band1 = call(analysis_columns_kernel, (image_start, wav_head, wav_rest), (own_shape,), "first_columns")[0]
    band0, part = call(
        functools.partial(rows_kernel, True),
        (odd_arg, image_start, near[:, :send], far[:, :send], mats),
        (tall_shape, part_shape), "first_rows", 1,
    )
    weight_sums = call(squares_kernel, (band0, band1), (sum_shape,), "squares")[0]
    grad = gradient(part)
    new, near, far = call(
        functools.partial(update_kernel, 0),
        (odd_arg, moved0, moved1, image_start, grad, wav_rows, wav_head_t, wav_rest_t),
        (own_shape, send_shape, send_shape), "first_update", 1,
    )
    dual0, dual1 = moved0, moved1
    estimate = new
    passes = OUTER * INNER
    radius = None
    for step in range(passes):
        near, far = exchange(near, far)
        band1, moved1, sum1 = call(
            columns_kernel, (estimate, wav_head, wav_rest, dual1, band1),
            (own_shape, own_shape, (height, width)), "columns",
        )
        band0, part, moved0, sums = call(
            functools.partial(rows_kernel, False),
            (odd_arg, estimate, near, far, mats, dual0, band0, sum1),
            (tall_shape, part_shape, tall_shape, sum_shape), "rows", 1,
        )
        if step % INNER == 0:
            terms = gathered(jnp.concatenate([sums, weight_sums], axis=0))
            weight_total = sum(term[sum_shape[0] :] for term in terms)
            terms = [term[: sum_shape[0]] for term in terms]
            radius = RADIUS_SCALE * total_chans / (jnp.sqrt(weight_total) + WEIGHT_OFFSET)
        else:
            terms = gathered(sums)
        if step % INNER == INNER - 1 and step + 1 < passes:
            weight_sums = call(squares_kernel, (band0, band1), (sum_shape,), "squares")[0]
        if step + 1 < passes:
            grad = gradient(part)
            estimate, near, far, dual0, dual1 = call(
                functools.partial(update_kernel, len(terms)),
                (odd_arg, *terms, radius, moved0, moved1, estimate, grad, wav_rows, wav_head_t, wav_rest_t),
                (own_shape, send_shape, send_shape, tall_shape, own_shape), "update", 1,
            )
        else:
            dual_final = call(
                functools.partial(final_kernel, len(terms)),
                (*terms, radius, moved0, moved1), ((chans, 2, height, width),), "final",
            )[0]
    return (estimate, dual_final)


def solution(mesh):
    return jax.shard_map(
        on_device,
        mesh=mesh,
        in_specs=(
            P("chan", "facet", None),
            P("chan", "facet", None),
            P("chan", None, "facet", None),
            P("chan", None),
            P("chan", None),
            P(),
            P("chan"),
        ),
        out_specs=(P("chan", "facet", None), P("chan", None, "facet", None)),
        check_vma=False,
    )
```

```python
import functools

import jax
import jax.numpy as jnp
from jax import lax
from jax.experimental import pallas as pl
from jax.experimental.pallas import tpu as pltpu
from jax.sharding import PartitionSpec as P

PSF_HALF = 8
WAV_HALF = 8
OUTER = 2
INNER = 3

STEP_PRIMAL = 0.9
STEP_DUAL = 0.2
RADIUS_SCALE = 0.06
WEIGHT_OFFSET = 1.0

F32 = jnp.float32
BF16 = jnp.bfloat16
VMEM_LIMIT = 24 * 1024 * 1024
PARAMS = pltpu.CompilerParams(vmem_limit_bytes=VMEM_LIMIT)


def split(values):
    head = values.astype(BF16)
    return head, (values - head.astype(F32)).astype(BF16)


def times_columns(values, head, rest):
    rows = values.shape[0]
    first, second = split(values)
    both = jnp.dot(jnp.concatenate([first, second], axis=0), head, preferred_element_type=F32)
    return both[:rows] + both[rows:] + jnp.dot(first, rest, preferred_element_type=F32)


def stacked(values):
    first, second = split(values)
    return jnp.concatenate([first, second, first], axis=0)


VM = pl.BlockSpec(memory_space=pltpu.VMEM)
SM = pl.BlockSpec(memory_space=pltpu.SMEM)


def call(kernel, ins, outs, name, scalars=0):
    return pl.pallas_call(
        kernel,
        out_shape=[jax.ShapeDtypeStruct(*shape) for shape in outs],
        in_specs=[SM] * scalars + [VM] * (len(ins) - scalars),
        out_specs=[VM] * len(outs),
        compiler_params=PARAMS,
        name=name,
    )(*ins)


def rows_kernel(odd_ref, own_ref, near_ref, far_ref, mats_ref, dual_ref, old_ref, sum1_ref, band_ref, part_ref, moved_ref, sums_ref):
    chans, height, width = own_ref.shape
    reach = band_ref.shape[1]
    odd = odd_ref[0] == 1

    def body(c, total):
        near, far = near_ref[c], far_ref[c]
        before, after = jnp.where(odd, near, far), jnp.where(odd, far, near)
        extended = jnp.concatenate([before, own_ref[c], after], axis=0)
        product = jnp.dot(mats_ref[c], stacked(extended), preferred_element_type=F32)
        band = product[:reach]
        band_ref[c] = band
        part_ref[c] = product[reach:]
        moved = dual_ref[c] + STEP_DUAL * (2.0 * band - old_ref[c])
        moved_ref[c] = moved
        return total + moved * moved

    total = lax.fori_loop(0, chans, body, jnp.zeros((reach, width), F32), unroll=2)
    sums_ref[:reach] = total
    sums_ref[reach:] = sum1_ref[...]


def first_rows_kernel(
    odd_ref, own_ref, near_ref, far_ref, mats_ref, start_ref, dirty_ref, sum1_ref,
    band_ref, part_ref, dual_ref, data_ref, sums_ref,
):
    chans, height, width = own_ref.shape
    reach = band_ref.shape[1]
    send, edge = (mats_ref.shape[2] // 3 - height) // 2, (reach - height) // 2
    odd = odd_ref[0] == 1

    def body(c, total):
        near, far = near_ref[c], far_ref[c]
        before, after = jnp.where(odd, near, far), jnp.where(odd, far, near)
        extended = jnp.concatenate([before[:send], own_ref[c], after[:send]], axis=0)
        product = jnp.dot(mats_ref[c], stacked(extended), preferred_element_type=F32)
        band = product[:reach]
        band_ref[c] = band
        part_ref[c] = product[reach:]
        at = send + edge
        dual_ref[c] = jnp.concatenate([before[send:at], start_ref[c, 0], after[send:at]], axis=0)
        data_ref[c] = jnp.concatenate([before[at:], dirty_ref[c], after[at:]], axis=0)
        return total + band * band

    total = lax.fori_loop(0, chans, body, jnp.zeros((reach, width), F32), unroll=2)
    sums_ref[:reach] = total
    sums_ref[reach:] = sum1_ref[...]


def squares_kernel(first_ref, second_ref, out_ref):
    low = first_ref.shape[1]
    out_ref[:low] = jnp.sum(first_ref[...] * first_ref[...], axis=0)
    out_ref[low:] = jnp.sum(second_ref[...] * second_ref[...], axis=0)


def pack_kernel(est_ref, dual_ref, dirty_ref, near_ref, far_ref, sems):
    chans, height, width = est_ref.shape
    total = near_ref.shape[1]
    send, edge = total // 2, total // 4
    odd = lax.rem(lax.axis_index("facet"), 2)
    copies = []
    for out_ref, low in ((near_ref, 1 - odd), (far_ref, odd)):
        at = 0
        for ref, rows in (
            (est_ref, send), (dual_ref.at[:, 0], edge), (dirty_ref, edge)
        ):
            start = pl.multiple_of(low * (height - rows), 8)
            copies.append(
                pltpu.make_async_copy(
                    ref.at[:, pl.ds(start, rows)], out_ref.at[:, at : at + rows], sems.at[len(copies)]
                )
            )
            at += rows
    for copy in copies:
        copy.start()
    for copy in copies:
        copy.wait()


LANES = 128


def banded(line, rows):
    return pltpu.roll(
        jnp.broadcast_to(line, (rows, LANES)), 0, 1, stride=1, stride_axis=0
    )


def square_band(line, width, half):
    around = banded(line, LANES)
    offset = lax.broadcasted_iota(jnp.int32, (LANES, LANES), 1) - lax.broadcasted_iota(
        jnp.int32, (LANES, LANES), 0
    )
    parts = []
    for piece in split(around):
        piece = piece.astype(F32)
        middle = jnp.where(jnp.abs(offset) <= half, piece, 0.0).astype(BF16)
        right = jnp.where(offset <= half - LANES, piece, 0.0).astype(BF16)
        left = jnp.where(offset >= LANES - half, piece, 0.0).astype(BF16)
        blank = jnp.zeros((LANES, LANES), BF16)
        tiles = width // LANES
        kinds = {0: middle, 1: right, -1: left}
        parts.append(
            jnp.concatenate(
                [
                    jnp.concatenate([kinds.get(j - i, blank) for j in range(tiles)], axis=1)
                    for i in range(tiles)
                ],
                axis=0,
            )
        )
    return parts


def matrices_kernel(
    flags_ref, lines_ref, mats_ref, adj_ref, wav_rows_ref,
    around_head_ref, around_rest_ref, back_head_ref, back_rest_ref,
    wav_head_ref, wav_rest_ref, wav_head_t_ref, wav_rest_t_ref,
):
    chans, width = around_head_ref.shape[:2]
    both, tall = mats_ref.shape[1], mats_ref.shape[2] // 3
    height, reach = wav_rows_ref.shape[0], wav_rows_ref.shape[1] // 3
    edge = (reach - height) // 2
    facet, facets = lax.axis_index("facet"), lax.axis_size("facet")

    def inside(shape, dim):
        at = lax.broadcasted_iota(jnp.int32, shape, dim)
        low = jnp.where(facet > 0, 0, edge)
        high = jnp.where(facet < facets - 1, reach, reach - edge)
        return jnp.where((at >= low) & (at < high), 1.0, 0.0)

    def line(c, k):
        return lines_ref[c, :, k * LANES : (k + 1) * LANES]

    def wide_rows(matrix):
        first, second = split(matrix)
        first, second = first.astype(F32), second.astype(F32)
        return jnp.concatenate([first, first, second], axis=1).astype(BF16)

    wav_head_ref[...], wav_rest_ref[...] = square_band(line(chans, 0), width, WAV_HALF)
    wav_head_t_ref[...], wav_rest_t_ref[...] = square_band(line(chans, 1), width, WAV_HALF)
    wav_rows_ref[...] = wide_rows(banded(line(chans, 3), height)[:, :reach])
    band = wide_rows((banded(line(chans, 2), reach) * inside((reach, LANES), 0))[:, :tall])

    def body(c, carry):
        head, rest = square_band(line(c, 0), width, PSF_HALF)
        back_head, back_rest = square_band(line(c, 1), width, PSF_HALF)
        back_head_ref[c] = back_head
        back_rest_ref[c] = back_rest
        around = (
            jnp.dot(head, back_head, preferred_element_type=F32)
            + jnp.dot(rest, back_head, preferred_element_type=F32)
            + jnp.dot(head, back_rest, preferred_element_type=F32)
        )
        around_head_ref[c], around_rest_ref[c] = split(around)
        flag = flags_ref[c].astype(F32)
        adjoint = banded(line(c, 3), height) * flag
        adj_ref[c] = wide_rows(adjoint[:, :reach])
        adjoint = adjoint * inside((height, LANES), 1)
        forward = banded(line(c, 2), reach)
        first, second = split(adjoint[:, :reach])
        head, rest = split(forward)
        normal = (
            jnp.dot(first, head, preferred_element_type=F32)
            + jnp.dot(second, head, preferred_element_type=F32)
            + jnp.dot(first, rest, preferred_element_type=F32)
        )
        mats_ref[c, :reach] = band
        mats_ref[c, reach:] = wide_rows(normal[:, :tall])
        return carry

    lax.fori_loop(0, chans, body, 0)


def columns_kernel(own_ref, head_ref, rest_ref, dual_ref, old_ref, band_ref, moved_ref, sum_ref):
    chans, height, width = own_ref.shape
    group = 8
    total = jnp.zeros((height, width), F32)
    for c in range(0, chans, group):
        n = min(group, chans - c)
        band = times_columns(
            own_ref[c : c + n].reshape(n * height, width), head_ref[...], rest_ref[...]
        ).reshape(n, height, width)
        band_ref[c : c + n] = band
        moved = dual_ref[c : c + n] + STEP_DUAL * (2.0 * band - old_ref[c : c + n])
        moved_ref[c : c + n] = moved
        total = total + jnp.sum(moved * moved, axis=0)
    sum_ref[...] = total


def first_columns_kernel(own_ref, head_ref, rest_ref, band_ref, sum_ref):
    chans, height, width = own_ref.shape
    group = 8
    total = jnp.zeros((height, width), F32)
    for c in range(0, chans, group):
        n = min(group, chans - c)
        band = times_columns(
            own_ref[c : c + n].reshape(n * height, width), head_ref[...], rest_ref[...]
        ).reshape(n, height, width)
        band_ref[c : c + n] = band
        total = total + jnp.sum(band * band, axis=0)
    sum_ref[...] = total


def first_gradient_kernel(
    part_ref, head_ref, rest_ref, dirty_ref, back_head_ref, back_rest_ref, adj_ref, data_ref, grad_ref
):
    chans = part_ref.shape[0]

    def body(c, carry):
        across = times_columns(dirty_ref[c], back_head_ref[c], back_rest_ref[c])
        data = jnp.dot(adj_ref[c], stacked(across), preferred_element_type=F32)
        data_ref[c] = data
        grad_ref[c] = times_columns(part_ref[c], head_ref[c], rest_ref[c]) - data
        return carry

    lax.fori_loop(0, chans, body, 0, unroll=2)


def gradient_kernel(part_ref, head_ref, rest_ref, data_ref, grad_ref):
    chans = part_ref.shape[0]

    def body(c, carry):
        grad_ref[c] = times_columns(part_ref[c], head_ref[c], rest_ref[c]) - data_ref[c]
        return carry

    lax.fori_loop(0, chans, body, 0, unroll=2)


def scaled(sums_refs, radius):
    total = sums_refs[0][...]
    for ref in sums_refs[1:]:
        total = total + ref[...]
    length = jnp.sqrt(total)
    return radius / jnp.maximum(length, radius)


def radius_kernel(factor, *refs):
    *sums_refs, out_ref = refs
    total = sums_refs[0][...]
    for ref in sums_refs[1:]:
        total = total + ref[...]
    out_ref[...] = factor / (jnp.sqrt(total) + WEIGHT_OFFSET)


def update_kernel(n_sums, odd_ref, *refs):
    sums_refs, refs = refs[:n_sums], refs[n_sums:]
    if n_sums:
        radius_ref, refs = refs[0], refs[1:]
    (
        moved0_ref, moved1_ref, own_ref, grad_ref, rows_ref, head_ref, rest_ref,
        new_ref, near_ref, far_ref, *duals,
    ) = refs
    chans, height, width = own_ref.shape
    reach = moved0_ref.shape[1]
    send = near_ref.shape[1]
    odd = odd_ref[0] == 1
    if n_sums:
        dual0_ref, dual1_ref = duals
        scale = scaled(sums_refs, radius_ref[...])
        scale0, scale1 = scale[:reach], scale[reach:]
    group = 4
    for c0 in range(0, chans, group):
        n = min(group, chans - c0)
        dual1 = moved1_ref[c0 : c0 + n]
        if n_sums:
            dual1 = dual1 * scale1[None]
            dual1_ref[c0 : c0 + n] = dual1
        across = times_columns(dual1.reshape(n * height, width), head_ref[...], rest_ref[...])
        for c in range(c0, c0 + n):
            dual0 = moved0_ref[c]
            if n_sums:
                dual0 = dual0 * scale0
                dual0_ref[c] = dual0
            down = jnp.dot(rows_ref[...], stacked(dual0), preferred_element_type=F32)
            at = (c - c0) * height
            step = grad_ref[c] + (down + across[at : at + height])
            new = jnp.maximum(own_ref[c] - STEP_PRIMAL * step, 0.0)
            new_ref[c] = new
            top, bottom = new[:send], new[height - send :]
            near_ref[c] = jnp.where(odd, top, bottom)
            far_ref[c] = jnp.where(odd, bottom, top)


def final_kernel(n_sums, *refs):
    sums_refs, refs = refs[:n_sums], refs[n_sums:]
    radius_ref, moved0_ref, moved1_ref, dual_ref = refs
    height = moved1_ref.shape[1]
    reach = moved0_ref.shape[1]
    pad = (reach - height) // 2
    scale = scaled(sums_refs, radius_ref[...])
    scale0, scale1 = scale[pad : pad + height], scale[reach:]
    for c in range(moved1_ref.shape[0]):
        dual_ref[c, 0] = moved0_ref[c, pad : pad + height] * scale0
        dual_ref[c, 1] = moved1_ref[c] * scale1


def exchange(near, far):
    n = lax.axis_size("facet")
    pair = [(i, i ^ 1) for i in range(n)]
    cross = [(i, ((i + 1) ^ 1) - 1) for i in range(n) if 0 <= ((i + 1) ^ 1) - 1 < n]
    return lax.ppermute(near, "facet", pair), lax.ppermute(far, "facet", cross)


def gathered(sums):
    n = lax.axis_size("chan")
    if n & (n - 1):
        return [lax.psum(sums, "chan")]
    low = 1
    terms = [sums]
    while low < n:
        radix = min(4, n // low)
        total = terms[0]
        for term in terms[1:]:
            total = total + term
        terms = [total] + [
            lax.ppermute(total, "chan", [(i, i ^ (k * low)) for i in range(n)])
            for k in range(1, radix)
        ]
        low *= radix
    return terms


def on_device(
    dirty_image, image_start, dual_start, psf_rows, psf_cols, wavelet_taps, channel_flags
):
    chans, height, width = image_start.shape
    total_chans = chans * lax.axis_size("chan")
    edge = max(PSF_HALF, WAV_HALF)
    reach, send = height + 2 * edge, 2 * edge
    tall = height + 2 * send
    passes = OUTER * INNER
    odd = (lax.axis_index("facet") % 2).astype(jnp.int32)[None]

    own = ((chans, height, width), F32)
    taller = ((chans, reach, width), F32)
    sides = ((chans, send, width), F32)
    summed = ((reach + height, width), F32)
    square = ((width, width), BF16)
    squares = ((chans, width, width), BF16)

    first_sides = ((chans, 2 * send, width), F32)
    near, far = pl.pallas_call(
        pack_kernel,
        out_shape=[jax.ShapeDtypeStruct(*first_sides)] * 2,
        in_specs=[pl.BlockSpec(memory_space=pltpu.HBM)] * 3,
        out_specs=[VM] * 2,
        scratch_shapes=[pltpu.SemaphoreType.DMA((6,))],
        compiler_params=PARAMS,
        name="pack",
    )(image_start, dual_start, dirty_image)
    near, far = exchange(near, far)

    def lines(cols, rows, half_c, half_r):
        def circle(taps, half):
            gap = jnp.zeros((taps.shape[0], LANES - 2 * half - 1), F32)
            return jnp.concatenate([taps[:, half:], gap, taps[:, :half]], axis=1)

        def ramp(taps, half):
            lead = jnp.zeros((taps.shape[0], edge - half), F32)
            gap = jnp.zeros((taps.shape[0], LANES - half - edge - 1), F32)
            return jnp.concatenate([lead, taps, gap], axis=1)

        return jnp.concatenate(
            [circle(cols[:, ::-1], half_c), circle(cols, half_c), ramp(rows, half_r), ramp(rows[:, ::-1], half_r)],
            axis=1,
        )

    table = jnp.concatenate(
        [
            lines(psf_cols, psf_rows, PSF_HALF, PSF_HALF),
            lines(wavelet_taps[1:2], wavelet_taps[0:1], WAV_HALF, WAV_HALF),
        ],
        axis=0,
    )
    (
        mats, adjoint, wav_rows, around_head, around_rest, back_head, back_rest,
        wav_head, wav_rest, wav_head_t, wav_rest_t,
    ) = call(
        matrices_kernel, (channel_flags, table[:, None]),
        (
            ((chans, reach + height, 3 * tall), BF16), ((chans, height, 3 * reach), BF16),
            ((height, 3 * reach), BF16), squares, squares, squares, squares,
            square, square, square, square,
        ),
        "matrices", 1,
    )
    band1, sum1 = call(
        first_columns_kernel, (image_start, wav_head, wav_rest), (own, ((height, width), F32)), "first_columns"
    )
    band0, part, dual0, dirty, weight_sums = call(
        first_rows_kernel, (odd, image_start, near, far, mats, dual_start, dirty_image, sum1),
        (taller, own, taller, taller, summed), "first_rows", 1,
    )
    data, grad = call(
        first_gradient_kernel,
        (part, around_head, around_rest, dirty, back_head, back_rest, adjoint), (own, own), "first_gradient",
    )
    dual1 = dual_start[:, 1]
    estimate, near, far = call(
        functools.partial(update_kernel, 0),
        (odd, dual0, dual1, image_start, grad, wav_rows, wav_head_t, wav_rest_t),
        (own, sides, sides), "first_update", 1,
    )
    for step in range(passes):
        near, far = exchange(near, far)
        if step % INNER == 0:
            terms = gathered(weight_sums)
        band1, moved1, sum1 = call(
            columns_kernel, (estimate, wav_head, wav_rest, dual1, band1),
            (own, own, ((height, width), F32)), "columns",
        )
        if step % INNER == 0:
            radius = call(
                functools.partial(radius_kernel, RADIUS_SCALE * total_chans), tuple(terms), (summed,), "radius"
            )[0]
        band0, part, moved0, sums = call(
            rows_kernel, (odd, estimate, near, far, mats, dual0, band0, sum1),
            (taller, own, taller, summed), "rows", 1,
        )
        terms = gathered(sums)
        if step % INNER == INNER - 1 and step + 1 < passes:
            weight_sums = call(squares_kernel, (band0, band1), (summed,), "squares")[0]
        if step + 1 < passes:
            grad = call(gradient_kernel, (part, around_head, around_rest, data), (own,), "gradient")[0]
            estimate, near, far, dual0, dual1 = call(
                functools.partial(update_kernel, len(terms)),
                (odd, *terms, radius, moved0, moved1, estimate, grad, wav_rows, wav_head_t, wav_rest_t),
                (own, sides, sides, taller, own), "update", 1,
            )
        else:
            dual_final = call(
                functools.partial(final_kernel, len(terms)), (*terms, radius, moved0, moved1),
                (((chans, 2, height, width), F32),), "final",
            )[0]
    return (estimate, dual_final)


def solution(mesh):
    return jax.shard_map(
        on_device,
        mesh=mesh,
        in_specs=(
            P("chan", "facet", None),
            P("chan", "facet", None),
            P("chan", None, "facet", None),
            P("chan", None),
            P("chan", None),
            P(),
            P("chan"),
        ),
        out_specs=(P("chan", "facet", None), P("chan", None, "facet", None)),
        check_vma=False,
    )
```

```python
import functools

import jax
import jax.numpy as jnp
from jax import lax
from jax.experimental import pallas as pl
from jax.experimental.pallas import tpu as pltpu
from jax.sharding import PartitionSpec as P

PSF_HALF = 8
WAV_HALF = 8
OUTER = 2
INNER = 3

STEP_PRIMAL = 0.9
STEP_DUAL = 0.2
RADIUS_SCALE = 0.06
WEIGHT_OFFSET = 1.0

F32 = jnp.float32
BF16 = jnp.bfloat16
LANES = 128
UNROLL = 4
GROUP = 8
VMEM_LIMIT = 24 * 1024 * 1024
PARAMS = pltpu.CompilerParams(vmem_limit_bytes=VMEM_LIMIT)


def split(values):
    head = values.astype(BF16)
    return head, (values - head.astype(F32)).astype(BF16)


def times_columns(values, head, rest):
    rows = values.shape[0]
    first, second = split(values)
    both = jnp.dot(jnp.concatenate([first, second], axis=0), head, preferred_element_type=F32)
    return both[:rows] + both[rows:] + jnp.dot(first, rest, preferred_element_type=F32)


def stacked(values):
    first, second = split(values)
    return jnp.concatenate([first, second, first], axis=0)


VM = pl.BlockSpec(memory_space=pltpu.VMEM)
SM = pl.BlockSpec(memory_space=pltpu.SMEM)


def call(kernel, ins, outs, name, scalars=0, aliases=None):
    return pl.pallas_call(
        kernel,
        out_shape=[jax.ShapeDtypeStruct(*shape) for shape in outs],
        in_specs=[SM] * scalars + [VM] * (len(ins) - scalars),
        out_specs=[VM] * len(outs),
        input_output_aliases=aliases or {},
        compiler_params=PARAMS,
        name=name,
    )(*ins)


def sided(odd, near, far, send):
    rows, width = near.shape
    if rows < send:
        blank = jnp.zeros((send - rows, width), F32)
        above = lambda rim: jnp.concatenate([blank, rim], axis=0)
        below = lambda rim: jnp.concatenate([rim, blank], axis=0)
        near = jnp.where(odd, above(near), below(near))
        far = jnp.where(odd, below(far), above(far))
    return near, far


def near_kernel(
    send, odd_ref, own_ref, near_ref, mats_ref, dual0_ref, old0_ref, head_ref, rest_ref, dual1_ref, old1_ref,
    band0_ref, part_ref, moved0_ref, band1_ref, moved1_ref, sums_ref,
):
    chans, height, width = own_ref.shape
    reach = band0_ref.shape[1]
    odd = odd_ref[0] == 1

    def body(c, total):
        near, _ = sided(odd, near_ref[c], near_ref[c], send)
        rows = jnp.concatenate([own_ref[c], near], axis=0)
        product = jnp.dot(mats_ref[c], stacked(rows), preferred_element_type=F32)
        band = product[:reach]
        band0_ref[c] = band
        part_ref[c] = product[reach:]
        moved = dual0_ref[c] + STEP_DUAL * (2.0 * band - old0_ref[c])
        moved0_ref[c] = moved
        return total + moved * moved

    sums_ref[:reach] = lax.fori_loop(0, chans, body, jnp.zeros((reach, width), F32), unroll=UNROLL)
    total = jnp.zeros((height, width), F32)
    for c in range(0, chans, GROUP):
        n = min(GROUP, chans - c)
        band = times_columns(
            own_ref[c : c + n].reshape(n * height, width), head_ref[...], rest_ref[...]
        ).reshape(n, height, width)
        band1_ref[c : c + n] = band
        moved = dual1_ref[c : c + n] + STEP_DUAL * (2.0 * band - old1_ref[c : c + n])
        moved1_ref[c : c + n] = moved
        total = total + jnp.sum(moved * moved, axis=0)
    sums_ref[reach:] = total


def far_kernel(send, odd_ref, far_ref, mats_ref, band_in_ref, moved_in_ref, sums_in_ref, band_ref, moved_ref, sums_ref):
    del band_in_ref, moved_in_ref
    chans, reach, width = band_ref.shape
    odd = odd_ref[0] == 1
    start = pl.multiple_of(odd_ref[0] * (reach - send), 16)
    touched = pl.ds(start, send)

    def body(c, total):
        _, far = sided(odd, far_ref[c], far_ref[c], send)
        product = jnp.dot(mats_ref[c, touched, :], stacked(far), preferred_element_type=F32)
        band_ref[c, touched, :] = band_ref[c, touched, :] + product
        moved = moved_ref[c, touched, :] + (2.0 * STEP_DUAL) * product
        moved_ref[c, touched, :] = moved
        return total + moved * moved

    sums_ref[...] = sums_in_ref[...]
    sums_ref[touched, :] = lax.fori_loop(0, chans, body, jnp.zeros((send, width), F32), unroll=UNROLL)


def first_rows_kernel(
    odd_ref, own_ref, near_ref, far_ref, mats_ref, far_mats_ref, start_ref, dirty_ref, sum1_ref,
    band_ref, part_ref, dual_ref, data_ref, sums_ref,
):
    chans, height, width = own_ref.shape
    reach = band_ref.shape[1]
    send, edge = far_mats_ref.shape[2] // 3, (reach - height) // 2
    odd = odd_ref[0] == 1

    def body(c, total):
        near, far = near_ref[c], far_ref[c]
        before, after = jnp.where(odd, near, far), jnp.where(odd, far, near)
        rows = jnp.concatenate([own_ref[c], near[:send]], axis=0)
        product = jnp.dot(mats_ref[c], stacked(rows), preferred_element_type=F32) + jnp.dot(
            far_mats_ref[c], stacked(far[:send]), preferred_element_type=F32
        )
        band = product[:reach]
        band_ref[c] = band
        part_ref[c] = product[reach:]
        at = send + edge
        dual_ref[c] = jnp.concatenate([before[send:at], start_ref[c, 0], after[send:at]], axis=0)
        data_ref[c] = jnp.concatenate([before[at:], dirty_ref[c], after[at:]], axis=0)
        return total + band * band

    sums_ref[:reach] = lax.fori_loop(0, chans, body, jnp.zeros((reach, width), F32), unroll=UNROLL)
    sums_ref[reach:] = sum1_ref[...]


def squares_kernel(first_ref, second_ref, out_ref):
    low = first_ref.shape[1]
    out_ref[:low] = jnp.sum(first_ref[...] * first_ref[...], axis=0)
    out_ref[low:] = jnp.sum(second_ref[...] * second_ref[...], axis=0)


def pack_kernel(est_ref, dual_ref, dirty_ref, near_ref, far_ref, sems):
    chans, height, width = est_ref.shape
    total = near_ref.shape[1]
    send, edge = total // 2, total // 4
    odd = lax.rem(lax.axis_index("facet"), 2)
    copies = []
    for out_ref, low in ((near_ref, 1 - odd), (far_ref, odd)):
        at = 0
        for ref, rows in (
            (est_ref, send), (dual_ref.at[:, 0], edge), (dirty_ref, edge)
        ):
            start = pl.multiple_of(low * (height - rows), 8)
            copies.append(
                pltpu.make_async_copy(
                    ref.at[:, pl.ds(start, rows)], out_ref.at[:, at : at + rows], sems.at[len(copies)]
                )
            )
            at += rows
    for copy in copies:
        copy.start()
    for copy in copies:
        copy.wait()


def banded(line, rows):
    return pltpu.roll(
        jnp.broadcast_to(line, (rows, LANES)), 0, 1, stride=1, stride_axis=0
    )


def square_band(line, width, half):
    around = banded(line, LANES)
    offset = lax.broadcasted_iota(jnp.int32, (LANES, LANES), 1) - lax.broadcasted_iota(
        jnp.int32, (LANES, LANES), 0
    )
    parts = []
    for piece in split(around):
        piece = piece.astype(F32)
        middle = jnp.where(jnp.abs(offset) <= half, piece, 0.0).astype(BF16)
        right = jnp.where(offset <= half - LANES, piece, 0.0).astype(BF16)
        left = jnp.where(offset >= LANES - half, piece, 0.0).astype(BF16)
        blank = jnp.zeros((LANES, LANES), BF16)
        tiles = width // LANES
        kinds = {0: middle, 1: right, -1: left}
        parts.append(
            jnp.concatenate(
                [
                    jnp.concatenate([kinds.get(j - i, blank) for j in range(tiles)], axis=1)
                    for i in range(tiles)
                ],
                axis=0,
            )
        )
    return parts


def matrices_kernel(
    flags_ref, lines_ref, mats_ref, far_mats_ref, adj_ref, wav_rows_ref,
    around_head_ref, around_rest_ref, back_head_ref, back_rest_ref,
    wav_head_ref, wav_rest_ref, wav_head_t_ref, wav_rest_t_ref,
):
    chans, width = around_head_ref.shape[:2]
    send = far_mats_ref.shape[2] // 3
    height, reach = wav_rows_ref.shape[0], wav_rows_ref.shape[1] // 3
    edge = (reach - height) // 2
    facet, facets = lax.axis_index("facet"), lax.axis_size("facet")
    odd = lax.rem(facet, 2) == 1

    def inside(shape, dim):
        at = lax.broadcasted_iota(jnp.int32, shape, dim)
        low = jnp.where(facet > 0, 0, edge)
        high = jnp.where(facet < facets - 1, reach, reach - edge)
        return jnp.where((at >= low) & (at < high), 1.0, 0.0)

    def line(c, k):
        return lines_ref[c, :, k * LANES : (k + 1) * LANES]

    def wide_rows(matrix):
        first, second = split(matrix)
        first, second = first.astype(F32), second.astype(F32)
        return jnp.concatenate([first, first, second], axis=1).astype(BF16)

    wav_head_ref[...], wav_rest_ref[...] = square_band(line(chans, 0), width, WAV_HALF)
    wav_head_t_ref[...], wav_rest_t_ref[...] = square_band(line(chans, 1), width, WAV_HALF)
    wav_rows_ref[...] = wide_rows(banded(line(chans, 3), height)[:, :reach])

    def by_side(matrix):
        low, own = matrix[:, :send], matrix[:, send : send + height]
        high = matrix[:, send + height : 2 * send + height]
        near, far = jnp.where(odd, low, high), jnp.where(odd, high, low)
        return wide_rows(jnp.concatenate([own, near], axis=1)), wide_rows(far)

    band, far_band = by_side(banded(line(chans, 2), reach) * inside((reach, LANES), 0))

    def body(c, carry):
        head, rest = square_band(line(c, 0), width, PSF_HALF)
        back_head, back_rest = square_band(line(c, 1), width, PSF_HALF)
        back_head_ref[c] = back_head
        back_rest_ref[c] = back_rest
        around = (
            jnp.dot(head, back_head, preferred_element_type=F32)
            + jnp.dot(rest, back_head, preferred_element_type=F32)
            + jnp.dot(head, back_rest, preferred_element_type=F32)
        )
        around_head_ref[c], around_rest_ref[c] = split(around)
        flag = flags_ref[c].astype(F32)
        adjoint = banded(line(c, 3), height) * flag
        adj_ref[c] = wide_rows(adjoint[:, :reach])
        adjoint = adjoint * inside((height, LANES), 1)
        forward = banded(line(c, 2), reach)
        first, second = split(adjoint[:, :reach])
        head, rest = split(forward)
        normal = (
            jnp.dot(first, head, preferred_element_type=F32)
            + jnp.dot(second, head, preferred_element_type=F32)
            + jnp.dot(first, rest, preferred_element_type=F32)
        )
        mats_ref[c, :reach] = band
        far_mats_ref[c, :reach] = far_band
        mats_ref[c, reach:], far_mats_ref[c, reach:] = by_side(normal)
        return carry

    lax.fori_loop(0, chans, body, 0, unroll=2)


def first_columns_kernel(own_ref, head_ref, rest_ref, band_ref, sum_ref):
    chans, height, width = own_ref.shape
    total = jnp.zeros((height, width), F32)
    for c in range(0, chans, GROUP):
        n = min(GROUP, chans - c)
        band = times_columns(
            own_ref[c : c + n].reshape(n * height, width), head_ref[...], rest_ref[...]
        ).reshape(n, height, width)
        band_ref[c : c + n] = band
        total = total + jnp.sum(band * band, axis=0)
    sum_ref[...] = total


def first_gradient_kernel(
    part_ref, head_ref, rest_ref, dirty_ref, back_head_ref, back_rest_ref, adj_ref, data_ref, grad_ref
):
    chans = part_ref.shape[0]

    def body(c, carry):
        across = times_columns(dirty_ref[c], back_head_ref[c], back_rest_ref[c])
        data = jnp.dot(adj_ref[c], stacked(across), preferred_element_type=F32)
        data_ref[c] = data
        grad_ref[c] = times_columns(part_ref[c], head_ref[c], rest_ref[c]) - data
        return carry

    lax.fori_loop(0, chans, body, 0, unroll=UNROLL)


def gradient_kernel(part_ref, far_ref, far_mats_ref, head_ref, rest_ref, data_ref, grad_ref):
    chans, height = part_ref.shape[:2]
    reach = far_mats_ref.shape[1] - height

    def body(c, carry):
        part = part_ref[c] + jnp.dot(
            far_mats_ref[c, reach:], stacked(far_ref[c]), preferred_element_type=F32
        )
        grad_ref[c] = times_columns(part, head_ref[c], rest_ref[c]) - data_ref[c]
        return carry

    lax.fori_loop(0, chans, body, 0, unroll=UNROLL)


def scaled(sums_refs, radius):
    total = sums_refs[0][...]
    for ref in sums_refs[1:]:
        total = total + ref[...]
    length = jnp.sqrt(total)
    return radius / jnp.maximum(length, radius)


def radius_kernel(factor, *refs):
    *sums_refs, out_ref = refs
    total = sums_refs[0][...]
    for ref in sums_refs[1:]:
        total = total + ref[...]
    out_ref[...] = factor / (jnp.sqrt(total) + WEIGHT_OFFSET)


def update_kernel(n_sums, odd_ref, *refs):
    sums_refs, refs = refs[:n_sums], refs[n_sums:]
    if n_sums:
        radius_ref, refs = refs[0], refs[1:]
    (
        moved0_ref, moved1_ref, own_ref, grad_ref, rows_ref, head_ref, rest_ref,
        new_ref, near_ref, far_ref, *duals,
    ) = refs
    chans, height, width = own_ref.shape
    reach = moved0_ref.shape[1]
    send = near_ref.shape[1]
    odd = odd_ref[0] == 1
    if n_sums:
        dual0_ref, dual1_ref = duals
        scale = scaled(sums_refs, radius_ref[...])
        scale0, scale1 = scale[:reach], scale[reach:]
    for c0 in range(0, chans, GROUP // 2):
        n = min(GROUP // 2, chans - c0)
        dual1 = moved1_ref[c0 : c0 + n]
        if n_sums:
            dual1 = dual1 * scale1[None]
            dual1_ref[c0 : c0 + n] = dual1
        across = times_columns(dual1.reshape(n * height, width), head_ref[...], rest_ref[...])
        for c in range(c0, c0 + n):
            dual0 = moved0_ref[c]
            if n_sums:
                dual0 = dual0 * scale0
                dual0_ref[c] = dual0
            down = jnp.dot(rows_ref[...], stacked(dual0), preferred_element_type=F32)
            at = (c - c0) * height
            step = grad_ref[c] + (down + across[at : at + height])
            new = jnp.maximum(own_ref[c] - STEP_PRIMAL * step, 0.0)
            new_ref[c] = new
            top, bottom = new[:send], new[height - send :]
            near_ref[c] = jnp.where(odd, top, bottom)
            far_ref[c] = jnp.where(odd, bottom, top)


def final_kernel(n_sums, *refs):
    sums_refs, refs = refs[:n_sums], refs[n_sums:]
    radius_ref, moved0_ref, moved1_ref, dual_ref = refs
    height = moved1_ref.shape[1]
    reach = moved0_ref.shape[1]
    pad = (reach - height) // 2
    scale = scaled(sums_refs, radius_ref[...])
    scale0, scale1 = scale[pad : pad + height], scale[reach:]
    for c in range(moved1_ref.shape[0]):
        dual_ref[c, 0] = moved0_ref[c, pad : pad + height] * scale0
        dual_ref[c, 1] = moved1_ref[c] * scale1


def publish_kernel(own_ref, _, out_ref, sem):
    copy = pltpu.make_async_copy(own_ref, out_ref, sem)
    copy.start()
    copy.wait()


def exchange(near, far):
    n = lax.axis_size("facet")
    pair = [(i, i ^ 1) for i in range(n)]
    cross = [(i, ((i + 1) ^ 1) - 1) for i in range(n) if 0 <= ((i + 1) ^ 1) - 1 < n]
    far = lax.ppermute(far, "facet", cross)
    return lax.ppermute(near, "facet", pair), far


def gathered(sums):
    n = lax.axis_size("chan")
    if n & (n - 1):
        return [lax.psum(sums, "chan")]
    low = 1
    terms = [sums]
    while low < n:
        radix = min(4, n // low)
        total = terms[0]
        for term in terms[1:]:
            total = total + term
        terms = [total] + [
            lax.ppermute(total, "chan", [(i, i ^ (k * low)) for i in range(n)])
            for k in sorted(range(1, radix), key=lambda k: -k.bit_count())
        ]
        low *= radix
    return terms


def on_device(
    dirty_image, image_start, dual_start, psf_rows, psf_cols, wavelet_taps, channel_flags
):
    chans, height, width = image_start.shape
    total_chans = chans * lax.axis_size("chan")
    edge = max(PSF_HALF, WAV_HALF)
    reach, send = height + 2 * edge, 2 * edge
    passes = OUTER * INNER
    odd = (lax.axis_index("facet") % 2).astype(jnp.int32)[None]

    own = ((chans, height, width), F32)
    taller = ((chans, reach, width), F32)
    sides = ((chans, send, width), F32)
    summed = ((reach + height, width), F32)
    square = ((width, width), BF16)
    squares = ((chans, width, width), BF16)

    first_sides = ((chans, 2 * send, width), F32)
    near, far = pl.pallas_call(
        pack_kernel,
        out_shape=[jax.ShapeDtypeStruct(*first_sides)] * 2,
        in_specs=[pl.BlockSpec(memory_space=pltpu.HBM)] * 3,
        out_specs=[VM] * 2,
        scratch_shapes=[pltpu.SemaphoreType.DMA((6,))],
        compiler_params=PARAMS,
        name="pack",
    )(*(pltpu.with_memory_space_constraint(x, pltpu.HBM) for x in (image_start, dual_start, dirty_image)))
    near, far = exchange(near, far)

    def lines(cols, rows, half_c, half_r):
        def circle(taps, half):
            gap = jnp.zeros((taps.shape[0], LANES - 2 * half - 1), F32)
            return jnp.concatenate([taps[:, half:], gap, taps[:, :half]], axis=1)

        def ramp(taps, half):
            lead = jnp.zeros((taps.shape[0], edge - half), F32)
            gap = jnp.zeros((taps.shape[0], LANES - half - edge - 1), F32)
            return jnp.concatenate([lead, taps, gap], axis=1)

        return jnp.concatenate(
            [circle(cols[:, ::-1], half_c), circle(cols, half_c), ramp(rows, half_r), ramp(rows[:, ::-1], half_r)],
            axis=1,
        )

    table = jnp.concatenate(
        [
            lines(psf_cols, psf_rows, PSF_HALF, PSF_HALF),
            lines(wavelet_taps[1:2], wavelet_taps[0:1], WAV_HALF, WAV_HALF),
        ],
        axis=0,
    )
    (
        mats, far_mats, adjoint, wav_rows, around_head, around_rest, back_head, back_rest,
        wav_head, wav_rest, wav_head_t, wav_rest_t,
    ) = call(
        matrices_kernel, (channel_flags, table[:, None]),
        (
            ((chans, reach + height, 3 * (height + send)), BF16), ((chans, reach + height, 3 * send), BF16),
            ((chans, height, 3 * reach), BF16),
            ((height, 3 * reach), BF16), squares, squares, squares, squares,
            square, square, square, square,
        ),
        "matrices", 1,
    )
    band1, sum1 = call(
        first_columns_kernel, (image_start, wav_head, wav_rest), (own, ((height, width), F32)), "first_columns"
    )
    band0, part, dual0, dirty, weight_sums = call(
        first_rows_kernel, (odd, image_start, near, far, mats, far_mats, dual_start, dirty_image, sum1),
        (taller, own, taller, taller, summed), "first_rows", 1,
    )
    data, grad = call(
        first_gradient_kernel,
        (part, around_head, around_rest, dirty, back_head, back_rest, adjoint), (own, own), "first_gradient",
    )
    dual1 = dual_start[:, 1]
    estimate, near, far = call(
        functools.partial(update_kernel, 0),
        (odd, dual0, dual1, image_start, grad, wav_rows, wav_head_t, wav_rest_t),
        (own, sides, sides), "first_update", 1,
    )
    for step in range(passes):
        near, far = exchange(near, far)
        if step % INNER == 0:
            terms = gathered(weight_sums)
        band0, part, moved0, band1, moved1, sums = call(
            functools.partial(near_kernel, send),
            (odd, estimate, near, mats, dual0, band0, wav_head, wav_rest, dual1, band1),
            (taller, own, taller, own, own, summed), "near", 1,
        )
        if step % INNER == 0:
            radius = call(
                functools.partial(radius_kernel, RADIUS_SCALE * total_chans), tuple(terms), (summed,), "radius"
            )[0]
        band0, moved0, sums = call(
            functools.partial(far_kernel, send), (odd, far, far_mats, band0, moved0, sums),
            (taller, taller, summed), "far", 1, {3: 0, 4: 1},
        )
        terms = gathered(sums)
        if step % INNER == INNER - 1 and step + 1 < passes:
            weight_sums = call(squares_kernel, (band0, band1), (summed,), "squares")[0]
        if step + 1 < passes:
            grad = call(
                gradient_kernel, (part, far, far_mats, around_head, around_rest, data), (own,), "gradient"
            )[0]
            rim = ((chans, send if step + 2 < passes else WAV_HALF, width), F32)
            estimate, near, far, dual0, dual1 = call(
                functools.partial(update_kernel, len(terms)),
                (odd, *terms, radius, moved0, moved1, estimate, grad, wav_rows, wav_head_t, wav_rest_t),
                (own, rim, rim, taller, own), "update", 1,
            )
        else:
            image_final = pl.pallas_call(
                publish_kernel,
                out_shape=jax.ShapeDtypeStruct(*own),
                in_specs=[VM, pl.BlockSpec(memory_space=pl.ANY)],
                out_specs=pl.BlockSpec(memory_space=pltpu.HBM),
                scratch_shapes=[pltpu.SemaphoreType.DMA],
                compiler_params=PARAMS,
                name="publish",
            )(estimate, sums)
            dual_final = call(
                functools.partial(final_kernel, len(terms)), (*terms, radius, moved0, moved1),
                (((chans, 2, height, width), F32),), "final",
            )[0]
    return (image_final, dual_final)


def solution(mesh):
    return jax.shard_map(
        on_device,
        mesh=mesh,
        in_specs=(
            P("chan", "facet", None),
            P("chan", "facet", None),
            P("chan", None, "facet", None),
            P("chan", None),
            P("chan", None),
            P(),
            P("chan"),
        ),
        out_specs=(P("chan", "facet", None), P("chan", None, "facet", None)),
        check_vma=False,
    )
```

```python
import functools

import jax
import jax.numpy as jnp
from jax import lax
from jax.experimental import pallas as pl
from jax.experimental.pallas import tpu as pltpu
from jax.sharding import PartitionSpec as P


PSF_HALF = 8
WAV_HALF = 8
OUTER = 2
INNER = 3

STEP_PRIMAL = 0.9
STEP_DUAL = 0.2
RADIUS_SCALE = 0.06
WEIGHT_OFFSET = 1.0


F32 = jnp.float32
BF16 = jnp.bfloat16
LANES = 128
UNROLL = 8
GROUP = 8
VMEM_LIMIT = 24 * 1024 * 1024
PARAMS = pltpu.CompilerParams(vmem_limit_bytes=VMEM_LIMIT)


def split(values):
    head = values.astype(BF16)
    return head, (values - head.astype(F32)).astype(BF16)


def times_columns(values, head, rest):
    rows = values.shape[0]
    first, second = split(values)
    both = jnp.dot(jnp.concatenate([first, second], axis=0), head, preferred_element_type=F32)
    return both[:rows] + both[rows:] + jnp.dot(first, rest, preferred_element_type=F32)


def stacked(values):
    first, second = split(values)
    return jnp.concatenate([first, second, first], axis=0)


VM = pl.BlockSpec(memory_space=pltpu.VMEM)
SM = pl.BlockSpec(memory_space=pltpu.SMEM)


def call(kernel, ins, outs, scalars=0, aliases=None):
    return pl.pallas_call(
        kernel,
        out_shape=[jax.ShapeDtypeStruct(*shape) for shape in outs],
        in_specs=[SM] * scalars + [VM] * (len(ins) - scalars),
        out_specs=[VM] * len(outs),
        input_output_aliases=aliases or {},
        compiler_params=PARAMS,
    )(*ins)


def padded(odd, far, send):
    rows, width = far.shape
    if rows < send:
        blank = jnp.zeros((send - rows, width), F32)
        below, above = jnp.concatenate([far, blank], axis=0), jnp.concatenate([blank, far], axis=0)
        far = jnp.where(odd, below, above)
    return far


def near_kernel(
    near_ref, far_ref, halo_ref, mats_ref, dual_u_ref, dual_t_ref, old_u_ref, old_t_ref,
    head_ref, rest_ref, dual1_ref, old1_ref, *refs,
):
    extra_ref = refs[0] if len(refs) > 8 else None
    band_u_ref, band_t_ref, part_ref, moved_u_ref, moved_t_ref, band1_ref, moved1_ref, sums_ref = refs[-8:]
    chans, half, width = near_ref.shape
    height, touched = 2 * half, band_t_ref.shape[1]
    free = band_u_ref.shape[1]

    def body(c, total):
        rows = jnp.concatenate([near_ref[c], far_ref[c], halo_ref[c]], axis=0)
        product = jnp.dot(mats_ref[c], stacked(rows), preferred_element_type=F32)
        band = product[:free]
        band_u_ref[c] = band
        moved = dual_u_ref[c] + STEP_DUAL * (2.0 * band - old_u_ref[c])
        moved_u_ref[c] = moved
        band_t = product[free : free + touched]
        band_t_ref[c] = band_t
        moved_t_ref[c] = dual_t_ref[c] + STEP_DUAL * (2.0 * band_t - old_t_ref[c])
        part_ref[c] = product[free + touched :]
        return total + moved * moved

    sums_ref[:free] = lax.fori_loop(0, chans, body, jnp.zeros((free, width), F32), unroll=UNROLL)
    total = jnp.zeros((height, width), F32)
    for c in range(0, chans, GROUP):
        n = min(GROUP, chans - c)
        rows = jnp.concatenate([near_ref[c : c + n], far_ref[c : c + n]], axis=1)
        band = times_columns(rows.reshape(n * height, width), head_ref[...], rest_ref[...])
        band = band.reshape(n, height, width)
        band1_ref[c : c + n] = band
        moved = dual1_ref[c : c + n] + STEP_DUAL * (2.0 * band - old1_ref[c : c + n])
        moved1_ref[c : c + n] = moved
        total = total + jnp.sum(moved * moved, axis=0)
    sums_ref[free : free + height] = total
    if extra_ref is not None:
        sums_ref[free + height :] = extra_ref[...]


def far_kernel(send, odd_ref, far_ref, mats_ref, band_in_ref, moved_in_ref, band_ref, moved_ref, sums_ref):
    chans, touched, width = band_ref.shape
    odd = odd_ref[0] == 1

    def body(c, total):
        far = padded(odd, far_ref[c], send)
        product = jnp.dot(mats_ref[...], stacked(far), preferred_element_type=F32)
        band_ref[c] = band_in_ref[c] + product
        moved = moved_in_ref[c] + (2.0 * STEP_DUAL) * product
        moved_ref[c] = moved
        return total + moved * moved

    sums_ref[...] = lax.fori_loop(0, chans, body, jnp.zeros((touched, width), F32), unroll=True)


def first_rows_kernel(
    odd_ref, near_ref, far_ref, halo_ref, far_halo_ref, mats_ref, far_band_ref, far_mats_ref, start_ref, dirty_ref,
    sum1_ref, band_u_ref, band_t_ref, part_ref, dual_u_ref, dual_t_ref, dual1_ref, data_ref, sums_ref,
):
    chans, half, width = near_ref.shape
    height, touched, free = 2 * half, band_t_ref.shape[1], band_u_ref.shape[1]
    reach = touched + free
    send, edge = far_mats_ref.shape[2] // 3, (reach - height) // 2
    odd = odd_ref[0] == 1

    def body(c, totals):
        near, far = halo_ref[c], far_halo_ref[c]
        before, after = jnp.where(odd, near, far), jnp.where(odd, far, near)
        rows = jnp.concatenate([near_ref[c], far_ref[c], near[:send]], axis=0)
        product = jnp.dot(mats_ref[c], stacked(rows), preferred_element_type=F32)
        far_rows = stacked(far[:send])
        band_t = product[free : free + touched] + jnp.dot(
            far_band_ref[...], far_rows, preferred_element_type=F32
        )
        band = product[:free]
        band_u_ref[c] = band
        band_t_ref[c] = band_t
        at = free + touched + half
        part_ref[c, :half] = product[free + touched : at]
        part_ref[c, half:] = product[at:] + jnp.dot(far_mats_ref[c], far_rows, preferred_element_type=F32)
        at = send + edge
        dual = jnp.concatenate([before[send:at], start_ref[c, 0], after[send:at]], axis=0)
        dual_u_ref[c] = jnp.where(odd, dual[:free], dual[touched:])
        dual_t_ref[c] = jnp.where(odd, dual[free:], dual[:touched])
        dual = start_ref[c, 1]
        dual1_ref[c, :half] = jnp.where(odd, dual[:half], dual[half:])
        dual1_ref[c, half:] = jnp.where(odd, dual[half:], dual[:half])
        data_ref[c] = jnp.concatenate([before[at:], dirty_ref[c], after[at:]], axis=0)
        return totals[0] + band * band, totals[1] + band_t * band_t

    zeros = jnp.zeros((free, width), F32), jnp.zeros((touched, width), F32)
    totals = lax.fori_loop(0, chans, body, zeros, unroll=UNROLL)
    sums_ref[:free] = totals[0]
    sums_ref[free : free + height] = sum1_ref[...]
    sums_ref[free + height :] = totals[1]


def squares_kernel(*refs):
    *band_refs, out_ref = refs
    at = 0
    for ref in band_refs:
        rows = ref.shape[1]
        out_ref[at : at + rows] = jnp.sum(ref[...] * ref[...], axis=0)
        at += rows


def pack_kernel(est_ref, dual_ref, dirty_ref, near_ref, far_ref, sems):
    _, height, _ = est_ref.shape
    total = near_ref.shape[1]
    send, edge = total // 2, total // 4
    odd = lax.rem(lax.axis_index("facet"), 2)
    copies = []
    for out_ref, low in ((near_ref, 1 - odd), (far_ref, odd)):
        at = 0
        for ref, rows in (
            (est_ref, send), (dual_ref.at[:, 0], edge), (dirty_ref, edge)
        ):
            start = pl.multiple_of(low * (height - rows), 8)
            copies.append(
                pltpu.make_async_copy(
                    ref.at[:, pl.ds(start, rows)], out_ref.at[:, at : at + rows], sems.at[len(copies)]
                )
            )
            at += rows
    for copy in copies:
        copy.start()
    for copy in copies:
        copy.wait()


def banded(line, rows):
    return pltpu.roll(
        jnp.broadcast_to(line, (rows, LANES)), 0, 1, stride=1, stride_axis=0
    )


def square_band(line, width, half):
    around = banded(line, LANES)
    offset = lax.broadcasted_iota(jnp.int32, (LANES, LANES), 1) - lax.broadcasted_iota(
        jnp.int32, (LANES, LANES), 0
    )
    parts = []
    for piece in split(around):
        piece = piece.astype(F32)
        middle = jnp.where(jnp.abs(offset) <= half, piece, 0.0).astype(BF16)
        right = jnp.where(offset <= half - LANES, piece, 0.0).astype(BF16)
        left = jnp.where(offset >= LANES - half, piece, 0.0).astype(BF16)
        blank = jnp.zeros((LANES, LANES), BF16)
        tiles = width // LANES
        kinds = {0: middle, 1: right, -1: left}
        parts.append(
            jnp.concatenate(
                [
                    jnp.concatenate([kinds.get(j - i, blank) for j in range(tiles)], axis=1)
                    for i in range(tiles)
                ],
                axis=0,
            )
        )
    return parts


def matrices_kernel(
    flags_ref, lines_ref, mats_ref, far_band_ref, far_mats_ref, adj_ref, wav_free_ref, wav_touched_ref,
    around_head_ref, around_rest_ref, back_head_ref, back_rest_ref,
    wav_head_ref, wav_rest_ref, wav_head_t_ref, wav_rest_t_ref,
):
    chans, width = around_head_ref.shape[:2]
    send = far_mats_ref.shape[2] // 3
    height, reach = adj_ref.shape[1], adj_ref.shape[2] // 3
    half, touched = height // 2, far_band_ref.shape[0]
    free = reach - touched
    edge = (reach - height) // 2
    facet, facets = lax.axis_index("facet"), lax.axis_size("facet")
    odd = lax.rem(facet, 2) == 1

    def inside(shape, dim):
        at = lax.broadcasted_iota(jnp.int32, shape, dim)
        low = jnp.where(facet > 0, 0, edge)
        high = jnp.where(facet < facets - 1, reach, reach - edge)
        return jnp.where((at >= low) & (at < high), 1.0, 0.0)

    def line(c, k):
        return lines_ref[c, :, k * LANES : (k + 1) * LANES]

    def wide_rows(matrix):
        first, second = split(matrix)
        first, second = first.astype(F32), second.astype(F32)
        return jnp.concatenate([first, first, second], axis=1).astype(BF16)

    wav_head_ref[...], wav_rest_ref[...] = square_band(line(chans, 0), width, WAV_HALF)
    wav_head_t_ref[...], wav_rest_t_ref[...] = square_band(line(chans, 1), width, WAV_HALF)

    def halves(matrix):
        low, high = matrix[:half], matrix[half:]
        return jnp.where(odd, low, high), jnp.where(odd, high, low)

    def reached(matrix):
        return jnp.where(odd, matrix[:free], matrix[touched:]), jnp.where(odd, matrix[free:], matrix[:touched])

    near, far = halves(banded(line(chans, 3), height)[:, :reach])
    wav_free_ref[...] = wide_rows(
        jnp.concatenate([jnp.where(odd, x[:, :free], x[:, touched:]) for x in (near, far)], axis=0)
    )
    wav_touched_ref[...] = wide_rows(jnp.where(odd, far[:, free:], far[:, :touched]))

    def by_side(matrix):
        low, high = matrix[:, :send], matrix[:, send + height : 2 * send + height]
        first, second = matrix[:, send : send + half], matrix[:, send + half : send + height]
        own = jnp.where(odd, first, second), jnp.where(odd, second, first)
        near, far = jnp.where(odd, low, high), jnp.where(odd, high, low)
        return wide_rows(jnp.concatenate([*own, near], axis=1)), wide_rows(far)

    band = banded(line(chans, 2), reach) * inside((reach, LANES), 0)
    band, far_band = by_side(jnp.concatenate(reached(band), axis=0))
    far_band_ref[...] = far_band[free:]

    def body(c, carry):
        head, rest = square_band(line(c, 0), width, PSF_HALF)
        back_head, back_rest = square_band(line(c, 1), width, PSF_HALF)
        back_head_ref[c] = back_head
        back_rest_ref[c] = back_rest
        around = (
            jnp.dot(head, back_head, preferred_element_type=F32)
            + jnp.dot(rest, back_head, preferred_element_type=F32)
            + jnp.dot(head, back_rest, preferred_element_type=F32)
        )
        around_head_ref[c], around_rest_ref[c] = split(around)
        flag = flags_ref[c].astype(F32)
        adjoint = banded(line(c, 3), height) * flag
        adjoint = jnp.concatenate(halves(adjoint), axis=0)
        adj_ref[c] = wide_rows(adjoint[:, :reach])
        adjoint = adjoint * inside((height, LANES), 1)
        forward = banded(line(c, 2), reach)
        first, second = split(adjoint[:, :reach])
        head, rest = split(forward)
        normal = (
            jnp.dot(first, head, preferred_element_type=F32)
            + jnp.dot(second, head, preferred_element_type=F32)
            + jnp.dot(first, rest, preferred_element_type=F32)
        )
        mats_ref[c, :reach] = band
        mats_ref[c, reach:], far = by_side(normal)
        far_mats_ref[c] = far[half:]
        return carry

    lax.fori_loop(0, chans, body, 0, unroll=2)


def first_columns_kernel(odd_ref, own_ref, head_ref, rest_ref, near_ref, far_ref, band_ref, sum_ref):
    chans, height, width = own_ref.shape
    half = height // 2
    odd = odd_ref[0] == 1
    total = jnp.zeros((height, width), F32)
    for c in range(0, chans, GROUP):
        n = min(GROUP, chans - c)
        low, high = own_ref[c : c + n, :half], own_ref[c : c + n, half:]
        near, far = jnp.where(odd, low, high), jnp.where(odd, high, low)
        near_ref[c : c + n] = near
        far_ref[c : c + n] = far
        rows = jnp.concatenate([near, far], axis=1)
        band = times_columns(rows.reshape(n * height, width), head_ref[...], rest_ref[...])
        band = band.reshape(n, height, width)
        band_ref[c : c + n] = band
        total = total + jnp.sum(band * band, axis=0)
    sum_ref[...] = total


def first_gradient_kernel(
    part_ref, head_ref, rest_ref, dirty_ref, back_head_ref, back_rest_ref, adj_ref, data_ref, grad_ref
):
    chans = part_ref.shape[0]

    def body(c, carry):
        across = times_columns(dirty_ref[c], back_head_ref[c], back_rest_ref[c])
        data = jnp.dot(adj_ref[c], stacked(across), preferred_element_type=F32)
        data_ref[c] = data
        grad_ref[c] = times_columns(part_ref[c], head_ref[c], rest_ref[c]) - data
        return carry

    lax.fori_loop(0, chans, body, 0, unroll=UNROLL)


def gradient_kernel(part_ref, halo_ref, far_mats_ref, head_ref, rest_ref, data_ref, _, grad_ref):
    chans, height = part_ref.shape[:2]
    half = height // 2

    def body(c, carry):
        far = jnp.dot(far_mats_ref[c], stacked(halo_ref[c]), preferred_element_type=F32)
        part = jnp.concatenate([part_ref[c, :half], part_ref[c, half:] + far], axis=0)
        grad_ref[c] = times_columns(part, head_ref[c], rest_ref[c]) - data_ref[c]
        return carry

    lax.fori_loop(0, chans, body, 0, unroll=UNROLL)


def scaled(sums_refs, rows, radius):
    total = sums_refs[0][:rows]
    for ref in sums_refs[1:]:
        total = total + ref[:rows]
    length = jnp.sqrt(total)
    return radius / jnp.maximum(length, radius)


def radius_kernel(factor, *refs):
    *sums_refs, out_ref = refs
    skip = sums_refs[0].shape[0] - out_ref.shape[0]
    total = sums_refs[0][skip:]
    for ref in sums_refs[1:]:
        total = total + ref[skip:]
    out_ref[...] = factor / (jnp.sqrt(total) + WEIGHT_OFFSET)


def early_kernel(n_sums, *refs):
    sums_refs, refs = refs[:n_sums], refs[n_sums:]
    (
        radius_ref, moved_u_ref, moved1_ref, near_ref, far_ref, grad_ref, rows_ref, head_ref, rest_ref,
        dual_u_ref, dual1_ref, new_near_ref, half_far_ref,
    ) = refs
    chans, half, width = near_ref.shape
    height, free = 2 * half, moved_u_ref.shape[1]
    scale = scaled(sums_refs, free + height, radius_ref[: free + height])
    scale_u, scale1 = scale[:free], scale[free:]
    for c0 in range(0, chans, GROUP // 2):
        n = min(GROUP // 2, chans - c0)
        dual1 = moved1_ref[c0 : c0 + n] * scale1[None]
        dual1_ref[c0 : c0 + n] = dual1
        across = times_columns(dual1.reshape(n * height, width), head_ref[...], rest_ref[...])
        for c in range(c0, c0 + n):
            dual = moved_u_ref[c] * scale_u
            dual_u_ref[c] = dual
            down = jnp.dot(rows_ref[...], stacked(dual), preferred_element_type=F32)
            at = (c - c0) * height
            step = STEP_PRIMAL * (grad_ref[c] + (down + across[at : at + height]))
            new_near_ref[c] = jnp.maximum(near_ref[c] - step[:half], 0.0)
            half_far_ref[c] = far_ref[c] - step[half:]


def late_kernel(n_sums, odd_ref, *refs):
    sums_refs, refs = refs[:n_sums], refs[n_sums:]
    radius_ref, moved_ref, half_far_ref, rows_ref, dual_ref, new_ref, *rim_refs = refs
    chans, touched = moved_ref.shape[:2]
    odd = odd_ref[0] == 1
    scale = scaled(sums_refs, touched, radius_ref[radius_ref.shape[0] - touched :])

    def body(c, carry):
        dual = moved_ref[c] * scale
        dual_ref[c] = dual
        down = jnp.dot(rows_ref[...], stacked(dual), preferred_element_type=F32)
        new = jnp.maximum(half_far_ref[c] - STEP_PRIMAL * down, 0.0)
        new_ref[c] = new
        for ref in rim_refs:
            rim = ref.shape[1]
            ref[c] = jnp.where(odd, new[new.shape[0] - rim :], new[:rim])
        return carry

    lax.fori_loop(0, chans, body, 0, unroll=True)


def first_update_kernel(
    dual_u_ref, dual_t_ref, dual1_ref, near_ref, far_ref, grad_ref, rows_ref, rows_t_ref, head_ref, rest_ref,
    new_near_ref, new_far_ref,
):
    chans, half, width = near_ref.shape
    height = 2 * half
    for c0 in range(0, chans, GROUP // 2):
        n = min(GROUP // 2, chans - c0)
        across = times_columns(
            dual1_ref[c0 : c0 + n].reshape(n * height, width), head_ref[...], rest_ref[...]
        )
        for c in range(c0, c0 + n):
            down = jnp.dot(rows_ref[...], stacked(dual_u_ref[c]), preferred_element_type=F32)
            late = jnp.dot(rows_t_ref[...], stacked(dual_t_ref[c]), preferred_element_type=F32)
            at = (c - c0) * height
            step = grad_ref[c] + (down + across[at : at + height])
            new_near_ref[c] = jnp.maximum(near_ref[c] - STEP_PRIMAL * step[:half], 0.0)
            new_far_ref[c] = jnp.maximum(far_ref[c] - STEP_PRIMAL * (step[half:] + late), 0.0)


def final_early_kernel(n_sums, odd_ref, *refs):
    sums_refs, refs = refs[:n_sums], refs[n_sums:]
    radius_ref, moved_u_ref, moved1_ref, dual_u_ref, out_ref, plane, sem = refs
    chans, height, _ = moved1_ref.shape
    half, free = height // 2, moved_u_ref.shape[1]
    odd = odd_ref[0] == 1
    scale = scaled(sums_refs, free + height, radius_ref[: free + height])
    for c in range(chans):
        dual_u_ref[c] = moved_u_ref[c] * scale[:free]
        dual = moved1_ref[c] * scale[free:]
        near, far = dual[:half], dual[half:]
        plane[c, :half] = jnp.where(odd, near, far)
        plane[c, half:] = jnp.where(odd, far, near)
    copy = pltpu.make_async_copy(plane, out_ref.at[:, 1], sem)
    copy.start()
    copy.wait()


def final_late_kernel(n_sums, odd_ref, *refs):
    sums_refs, refs = refs[:n_sums], refs[n_sums:]
    radius_ref, moved_ref, dual_u_ref, _, out_ref, plane, sems = refs
    chans, height, _ = plane.shape
    touched, free = moved_ref.shape[1], dual_u_ref.shape[1]
    edge = (touched + free - height) // 2
    odd = odd_ref[0] == 1
    scale = scaled(sums_refs, touched, radius_ref[radius_ref.shape[0] - touched :])
    group = chans // sems.shape[0]
    copies = []
    for c in range(chans):
        dual = moved_ref[c] * scale
        above = jnp.concatenate([dual_u_ref[c, edge:], dual[: touched - edge]], axis=0)
        below = jnp.concatenate([dual[edge:], dual_u_ref[c, : free - edge]], axis=0)
        plane[c] = jnp.where(odd, above, below)
        if (c + 1) % group == 0:
            part = slice(c + 1 - group, c + 1)
            copies.append(
                pltpu.make_async_copy(plane.at[part], out_ref.at[part, 0], sems.at[len(copies)])
            )
            copies[-1].start()
    for copy in copies:
        copy.wait()


def publish_kernel(near_ref, far_ref, _, out_ref, sems):
    half = near_ref.shape[1]
    odd = lax.rem(lax.axis_index("facet"), 2)
    copies = [
        pltpu.make_async_copy(
            ref, out_ref.at[:, pl.ds(pl.multiple_of(low * half, 8), half)], sems.at[k]
        )
        for k, (ref, low) in enumerate(((near_ref, 1 - odd), (far_ref, odd)))
    ]
    for copy in copies:
        copy.start()
    for copy in copies:
        copy.wait()


def trade(values, across):
    n = lax.axis_size("facet")
    if across:
        pairs = [(i, ((i + 1) ^ 1) - 1) for i in range(n) if 0 <= ((i + 1) ^ 1) - 1 < n]
    else:
        pairs = [(i, i ^ 1) for i in range(n)]
    return lax.ppermute(values, "facet", pairs)


def peers(n, low):
    return sorted(range(1, min(4, n // low)), key=lambda k: -k.bit_count())


def gathered(sums):
    n = lax.axis_size("chan")
    if n & (n - 1):
        return [lax.psum(sums, "chan")]
    low = 1
    terms = [sums]
    while low < n:
        total = terms[0]
        for term in terms[1:]:
            total = total + term
        terms = [total]
        for k in peers(n, low):
            terms.append(lax.ppermute(total, "chan", [(i, i ^ (k * low)) for i in range(n)]))
        low *= min(4, n // low)
    return terms


def on_device(
    dirty_image, image_start, dual_start, psf_rows, psf_cols, wavelet_taps, channel_flags
):
    chans, height, width = image_start.shape
    total_chans = chans * lax.axis_size("chan")
    edge = max(PSF_HALF, WAV_HALF)
    reach, send = height + 2 * edge, 2 * edge
    passes = OUTER * INNER
    odd = (lax.axis_index("facet") % 2).astype(jnp.int32)[None]

    half, touched = height // 2, send
    free = reach - touched
    if half != send:
        raise ValueError("facet height")

    def rows(count):
        return (chans, count, width), F32

    own, side, wavy, late_rows = rows(height), rows(half), rows(free), rows(touched)
    late_sum = ((touched, width), F32)
    summed = ((reach + height, width), F32)
    square = ((width, width), BF16)
    squares = ((chans, width, width), BF16)

    first_sides = rows(2 * send)
    near, far = pl.pallas_call(
        pack_kernel,
        out_shape=[pltpu.VMEM(*first_sides)] * 2,
        in_specs=[pl.BlockSpec(memory_space=pltpu.HBM)] * 3,
        out_specs=[VM] * 2,
        scratch_shapes=[pltpu.SemaphoreType.DMA((6,))],
        compiler_params=PARAMS,
        name="pack",
    )(*(pltpu.with_memory_space_constraint(x, pltpu.HBM) for x in (image_start, dual_start, dirty_image)))
    far, near = trade(far, True), trade(near, False)

    def lines(cols, rows, half_c, half_r):
        def circle(taps, half):
            gap = jnp.zeros((taps.shape[0], LANES - 2 * half - 1), F32)
            return jnp.concatenate([taps[:, half:], gap, taps[:, :half]], axis=1)

        def ramp(taps, half):
            lead = jnp.zeros((taps.shape[0], edge - half), F32)
            gap = jnp.zeros((taps.shape[0], LANES - half - edge - 1), F32)
            return jnp.concatenate([lead, taps, gap], axis=1)

        return jnp.concatenate(
            [circle(cols[:, ::-1], half_c), circle(cols, half_c), ramp(rows, half_r), ramp(rows[:, ::-1], half_r)],
            axis=1,
        )

    table = jnp.concatenate(
        [
            lines(psf_cols, psf_rows, PSF_HALF, PSF_HALF),
            lines(wavelet_taps[1:2], wavelet_taps[0:1], WAV_HALF, WAV_HALF),
        ],
        axis=0,
    )
    (
        mats, far_band, far_mats, adjoint, wav_free, wav_touched, around_head, around_rest, back_head, back_rest,
        wav_head, wav_rest, wav_head_t, wav_rest_t,
    ) = call(
        matrices_kernel, (channel_flags, table[:, None]),
        (
            ((chans, reach + height, 3 * (height + send)), BF16), ((touched, 3 * send), BF16),
            ((chans, half, 3 * send), BF16), ((chans, height, 3 * reach), BF16),
            ((height, 3 * free), BF16), ((half, 3 * touched), BF16),
            squares, squares, squares, squares, square, square, square, square,
        ),
        1,
    )
    est_near, est_far, band1, sum1 = call(
        first_columns_kernel, (odd, image_start, wav_head, wav_rest),
        (side, side, own, ((height, width), F32)), 1,
    )
    band_u, band_t, part, dual_u, dual_t, dual1, dirty, weight_sums = call(
        first_rows_kernel,
        (odd, est_near, est_far, near, far, mats, far_band, far_mats, dual_start, dirty_image, sum1),
        (wavy, late_rows, own, wavy, late_rows, own, rows(reach), summed), 1,
    )
    data, grad = call(
        first_gradient_kernel,
        (part, around_head, around_rest, dirty, back_head, back_rest, adjoint), (own, own),
    )
    est_near, est_far = call(
        first_update_kernel,
        (dual_u, dual_t, dual1, est_near, est_far, grad, wav_free, wav_touched, wav_head_t, wav_rest_t),
        (side, side),
    )
    rim = est_far
    near = trade(est_near, False)
    for step in range(passes):
        last = step + 1 == passes
        far = trade(rim, True)
        weigh = step % INNER == 0
        band_u, band_t, part, moved_u, moved_t, band1, moved1, sums = call(
            near_kernel,
            (est_near, est_far, near, mats, dual_u, dual_t, band_u, band_t, wav_head, wav_rest, dual1, band1)
            + ((weight_sums,) if weigh else ()),
            (
                wavy, late_rows, own, wavy, late_rows, own, own,
                ((free + height + (summed[0][0] if weigh else 0), width), F32),
            ),
        )
        early = gathered(sums)
        if weigh:
            radius = call(functools.partial(radius_kernel, RADIUS_SCALE * total_chans), tuple(early), (summed,))[0]
        band_t, moved_t, sums = call(
            functools.partial(far_kernel, send), (odd, far, far_band, band_t, moved_t),
            (late_rows, late_rows, late_sum), 1,
        )
        late = gathered(sums)
        if last:
            image_final = pl.pallas_call(
                publish_kernel,
                out_shape=jax.ShapeDtypeStruct(*own),
                in_specs=[VM, VM, pl.BlockSpec(memory_space=pl.ANY)],
                out_specs=pl.BlockSpec(memory_space=pltpu.HBM),
                scratch_shapes=[pltpu.SemaphoreType.DMA((2,))],
                compiler_params=PARAMS,
                name="publish",
            )(est_near, est_far, sums)
            in_hbm = pl.BlockSpec(memory_space=pltpu.HBM)
            result = jax.ShapeDtypeStruct((chans, 2, height, width), F32)
            dual_u, dual_final = pl.pallas_call(
                functools.partial(final_early_kernel, len(early)),
                out_shape=[jax.ShapeDtypeStruct(*wavy), result],
                in_specs=[SM] + [VM] * (len(early) + 3),
                out_specs=[VM, in_hbm],
                scratch_shapes=[pltpu.VMEM(*own), pltpu.SemaphoreType.DMA],
                compiler_params=PARAMS,
                name="final_early",
            )(odd, *early, radius, moved_u, moved1)
            dual_final = pl.pallas_call(
                functools.partial(final_late_kernel, len(late)),
                out_shape=result,
                in_specs=[SM] + [VM] * (len(late) + 3) + [in_hbm],
                out_specs=in_hbm,
                scratch_shapes=[pltpu.VMEM(*own), pltpu.SemaphoreType.DMA((4,))],
                input_output_aliases={len(late) + 4: 0},
                compiler_params=PARAMS,
                name="final_late",
            )(odd, *late, radius, moved_t, dual_u, dual_final)
            break
        grad = call(gradient_kernel, (part, far, far_mats, around_head, around_rest, data, sums), (own,))[0]
        dual_u, dual1, est_near, half_far = call(
            functools.partial(early_kernel, len(early)),
            (*early, radius, moved_u, moved1, est_near, est_far, grad, wav_free, wav_head_t, wav_rest_t),
            (wavy, own, side, side),
        )
        near = trade(est_near, False)
        if step % INNER == INNER - 1:
            weight_sums = call(squares_kernel, (band_u, band1, band_t), (summed,))[0]
        small = step + 2 == passes
        dual_t, est_far, *rims = call(
            functools.partial(late_kernel, len(late)),
            (odd, *late, radius, moved_t, half_far, wav_touched),
            (late_rows, side) + ((rows(WAV_HALF),) if small else ()), 1,
        )
        rim = rims[0] if small else est_far
    return (image_final, dual_final)


def solution(mesh):
    return jax.shard_map(
        on_device,
        mesh=mesh,
        in_specs=(
            P("chan", "facet", None),
            P("chan", "facet", None),
            P("chan", None, "facet", None),
            P("chan", None),
            P("chan", None),
            P(),
            P("chan"),
        ),
        out_specs=(P("chan", "facet", None), P("chan", None, "facet", None)),
        check_vma=False,
    )
```

```python
import functools

import jax
import jax.numpy as jnp
from jax import lax
from jax.experimental import pallas as pl
from jax.experimental.pallas import tpu as pltpu
from jax.sharding import PartitionSpec as P


PSF_HALF = 8
WAV_HALF = 8
OUTER = 2
INNER = 3

STEP_PRIMAL = 0.9
STEP_DUAL = 0.2
RADIUS_SCALE = 0.06
WEIGHT_OFFSET = 1.0


F32 = jnp.float32
BF16 = jnp.bfloat16
LANES = 128
GROUP = 8
VMEM_LIMIT = 24 * 1024 * 1024
PARAMS = pltpu.CompilerParams(vmem_limit_bytes=VMEM_LIMIT)


def split(values):
    head = values.astype(BF16)
    return head, (values - head.astype(F32)).astype(BF16)


def times_columns(values, head, rest):
    rows = values.shape[0]
    first, second = split(values)
    both = jnp.dot(jnp.concatenate([first, second], axis=0), head, preferred_element_type=F32)
    return both[:rows] + both[rows:] + jnp.dot(first, rest, preferred_element_type=F32)


def stacked(values):
    first, second = split(values)
    return jnp.concatenate([first, second, first], axis=0)


VM = pl.BlockSpec(memory_space=pltpu.VMEM)
SM = pl.BlockSpec(memory_space=pltpu.SMEM)


def call(kernel, ins, outs, scalars=0, aliases=None):
    return pl.pallas_call(
        kernel,
        out_shape=[jax.ShapeDtypeStruct(*shape) for shape in outs],
        in_specs=[SM] * scalars + [VM] * (len(ins) - scalars),
        out_specs=[VM] * len(outs),
        input_output_aliases=aliases or {},
        compiler_params=PARAMS,
    )(*ins)


def padded(odd, far, send):
    rows, width = far.shape
    if rows < send:
        blank = jnp.zeros((send - rows, width), F32)
        below, above = jnp.concatenate([far, blank], axis=0), jnp.concatenate([blank, far], axis=0)
        far = jnp.where(odd, below, above)
    return far


def near_kernel(
    weigh, last, near_ref, far_ref, halo_ref, mats_ref, dual_u_ref, dual_t_ref, old_u_ref, old_t_ref,
    head_ref, rest_ref, dual1_ref, old1_ref, *refs,
):
    refs = list(refs)
    extra_ref = refs.pop(0) if weigh else None
    moved_u_ref, moved_t_ref, moved1_ref, sums_ref = refs[:4]
    chans, half, width = near_ref.shape
    height, touched = 2 * half, moved_t_ref.shape[1]
    free = moved_u_ref.shape[1]

    def body(c, total):
        rows = jnp.concatenate([near_ref[c], far_ref[c], halo_ref[c]], axis=0)
        product = jnp.dot(mats_ref[c], stacked(rows), preferred_element_type=F32)
        band = product[:free]
        moved = dual_u_ref[c] + STEP_DUAL * (2.0 * band - old_u_ref[c])
        moved_u_ref[c] = moved
        band_t = product[free : free + touched]
        moved_t_ref[c] = dual_t_ref[c] + STEP_DUAL * (2.0 * band_t - old_t_ref[c])
        if not last:
            band_u_ref, band_t_ref, part_ref, _ = refs[4:]
            band_u_ref[c] = band
            band_t_ref[c] = band_t
            part_ref[c] = product[free + touched :]
        return total + moved * moved

    sums_ref[:free] = lax.fori_loop(0, chans, body, jnp.zeros((free, width), F32), unroll=True)
    total = jnp.zeros((height, width), F32)
    for c in range(0, chans, GROUP):
        n = min(GROUP, chans - c)
        rows = jnp.concatenate([near_ref[c : c + n], far_ref[c : c + n]], axis=1)
        band = times_columns(rows.reshape(n * height, width), head_ref[...], rest_ref[...])
        band = band.reshape(n, height, width)
        if not last:
            refs[7][c : c + n] = band
        moved = dual1_ref[c : c + n] + STEP_DUAL * (2.0 * band - old1_ref[c : c + n])
        moved1_ref[c : c + n] = moved
        total = total + jnp.sum(moved * moved, axis=0)
    sums_ref[free : free + height] = total
    if extra_ref is not None:
        sums_ref[free + height :] = extra_ref[...]


def far_kernel(send, odd_ref, far_ref, mats_ref, band_in_ref, moved_in_ref, moved_ref, sums_ref, *band_refs):
    chans, touched, width = moved_ref.shape
    odd = odd_ref[0] == 1

    def body(c, total):
        far = padded(odd, far_ref[c], send)
        product = jnp.dot(mats_ref[...], stacked(far), preferred_element_type=F32)
        for band_ref in band_refs:
            band_ref[c] = band_in_ref[c] + product
        moved = moved_in_ref[c] + (2.0 * STEP_DUAL) * product
        moved_ref[c] = moved
        return total + moved * moved

    sums_ref[...] = lax.fori_loop(0, chans, body, jnp.zeros((touched, width), F32), unroll=True)


def first_rows_kernel(
    odd_ref, near_ref, far_ref, halo_ref, far_halo_ref, mats_ref, far_band_ref, far_mats_ref, start_ref, dirty_ref,
    sum1_ref, band_u_ref, band_t_ref, part_ref, dual_u_ref, dual_t_ref, dual1_ref, data_ref, sums_ref,
):
    chans, half, width = near_ref.shape
    height, touched, free = 2 * half, band_t_ref.shape[1], band_u_ref.shape[1]
    reach = touched + free
    send, edge = far_mats_ref.shape[2] // 3, (reach - height) // 2
    odd = odd_ref[0] == 1

    def body(c, totals):
        near, far = halo_ref[c], far_halo_ref[c]
        before, after = jnp.where(odd, near, far), jnp.where(odd, far, near)
        rows = jnp.concatenate([near_ref[c], far_ref[c], near[:send]], axis=0)
        product = jnp.dot(mats_ref[c], stacked(rows), preferred_element_type=F32)
        far_rows = stacked(far[:send])
        band_t = product[free : free + touched] + jnp.dot(
            far_band_ref[...], far_rows, preferred_element_type=F32
        )
        band = product[:free]
        band_u_ref[c] = band
        band_t_ref[c] = band_t
        at = free + touched + half
        part_ref[c, :half] = product[free + touched : at]
        part_ref[c, half:] = product[at:] + jnp.dot(far_mats_ref[c], far_rows, preferred_element_type=F32)
        at = send + edge
        dual = jnp.concatenate([before[send:at], start_ref[c, 0], after[send:at]], axis=0)
        dual_u_ref[c] = jnp.where(odd, dual[:free], dual[touched:])
        dual_t_ref[c] = jnp.where(odd, dual[free:], dual[:touched])
        dual = start_ref[c, 1]
        dual1_ref[c, :half] = jnp.where(odd, dual[:half], dual[half:])
        dual1_ref[c, half:] = jnp.where(odd, dual[half:], dual[:half])
        data_ref[c] = jnp.concatenate([before[at:], dirty_ref[c], after[at:]], axis=0)
        return totals[0] + band * band, totals[1] + band_t * band_t

    zeros = jnp.zeros((free, width), F32), jnp.zeros((touched, width), F32)
    totals = lax.fori_loop(0, chans, body, zeros, unroll=True)
    sums_ref[:free] = totals[0]
    sums_ref[free : free + height] = sum1_ref[...]
    sums_ref[free + height :] = totals[1]


def squares_kernel(*refs):
    *band_refs, out_ref = refs
    at = 0
    for ref in band_refs:
        rows = ref.shape[1]
        out_ref[at : at + rows] = jnp.sum(ref[...] * ref[...], axis=0)
        at += rows


def pack_kernel(est_ref, dual_ref, dirty_ref, far_ref, near_ref, far_rows, near_rows, in_sems, out_sems):
    height = est_ref.shape[1]
    total = near_ref.shape[1]
    send, edge = total // 2, total // 4
    odd = lax.rem(lax.axis_index("facet"), 2)
    loads, stores = [], []
    for out_ref, held, low in ((far_ref, far_rows, odd), (near_ref, near_rows, 1 - odd)):
        at = 0
        for ref, rows in ((est_ref, send), (dual_ref.at[:, 0], edge), (dirty_ref, edge)):
            start = pl.multiple_of(low * (height - rows), 8)
            k = len(loads)
            piece = (slice(None), slice(at, at + rows))
            loads.append(pltpu.make_async_copy(ref.at[:, pl.ds(start, rows)], held.at[piece], in_sems.at[k]))
            stores.append(pltpu.make_async_copy(held.at[piece], out_ref.at[piece], out_sems.at[k]))
            at += rows
    for load in loads:
        load.start()
    for load, store in zip(loads, stores):
        load.wait()
        store.start()
    for store in stores:
        store.wait()


def banded(line, rows):
    return pltpu.roll(
        jnp.broadcast_to(line, (rows, LANES)), 0, 1, stride=1, stride_axis=0
    )


def square_band(line, width, half):
    around = banded(line, LANES)
    offset = lax.broadcasted_iota(jnp.int32, (LANES, LANES), 1) - lax.broadcasted_iota(
        jnp.int32, (LANES, LANES), 0
    )
    parts = []
    for piece in split(around):
        piece = piece.astype(F32)
        middle = jnp.where(jnp.abs(offset) <= half, piece, 0.0).astype(BF16)
        right = jnp.where(offset <= half - LANES, piece, 0.0).astype(BF16)
        left = jnp.where(offset >= LANES - half, piece, 0.0).astype(BF16)
        blank = jnp.zeros((LANES, LANES), BF16)
        tiles = width // LANES
        kinds = {0: middle, 1: right, -1: left}
        parts.append(
            jnp.concatenate(
                [
                    jnp.concatenate([kinds.get(j - i, blank) for j in range(tiles)], axis=1)
                    for i in range(tiles)
                ],
                axis=0,
            )
        )
    return parts


def matrices_kernel(
    flags_ref, lines_ref, mats_ref, far_band_ref, far_mats_ref, adj_ref, wav_free_ref, wav_touched_ref,
    around_head_ref, around_rest_ref, back_head_ref, back_rest_ref,
    wav_head_ref, wav_rest_ref, wav_head_t_ref, wav_rest_t_ref,
):
    chans, width = around_head_ref.shape[:2]
    send = far_mats_ref.shape[2] // 3
    height, reach = adj_ref.shape[1], adj_ref.shape[2] // 3
    half, touched = height // 2, far_band_ref.shape[0]
    free = reach - touched
    edge = (reach - height) // 2
    facet, facets = lax.axis_index("facet"), lax.axis_size("facet")
    odd = lax.rem(facet, 2) == 1

    def inside(shape, dim):
        at = lax.broadcasted_iota(jnp.int32, shape, dim)
        low = jnp.where(facet > 0, 0, edge)
        high = jnp.where(facet < facets - 1, reach, reach - edge)
        return jnp.where((at >= low) & (at < high), 1.0, 0.0)

    def line(c, k):
        return lines_ref[c, :, k * LANES : (k + 1) * LANES]

    def wide_rows(matrix):
        first, second = split(matrix)
        first, second = first.astype(F32), second.astype(F32)
        return jnp.concatenate([first, first, second], axis=1).astype(BF16)

    wav_head_ref[...], wav_rest_ref[...] = square_band(line(chans, 0), width, WAV_HALF)
    wav_head_t_ref[...], wav_rest_t_ref[...] = square_band(line(chans, 1), width, WAV_HALF)

    def halves(matrix):
        low, high = matrix[:half], matrix[half:]
        return jnp.where(odd, low, high), jnp.where(odd, high, low)

    def reached(matrix):
        return jnp.where(odd, matrix[:free], matrix[touched:]), jnp.where(odd, matrix[free:], matrix[:touched])

    near, far = halves(banded(line(chans, 3), height)[:, :reach])
    wav_free_ref[...] = wide_rows(
        jnp.concatenate([jnp.where(odd, x[:, :free], x[:, touched:]) for x in (near, far)], axis=0)
    )
    wav_touched_ref[...] = wide_rows(jnp.where(odd, far[:, free:], far[:, :touched]))

    def by_side(matrix):
        low, high = matrix[:, :send], matrix[:, send + height : 2 * send + height]
        first, second = matrix[:, send : send + half], matrix[:, send + half : send + height]
        own = jnp.where(odd, first, second), jnp.where(odd, second, first)
        near, far = jnp.where(odd, low, high), jnp.where(odd, high, low)
        return wide_rows(jnp.concatenate([*own, near], axis=1)), wide_rows(far)

    band = banded(line(chans, 2), reach) * inside((reach, LANES), 0)
    band, far_band = by_side(jnp.concatenate(reached(band), axis=0))
    far_band_ref[...] = far_band[free:]

    def body(c, carry):
        head, rest = square_band(line(c, 0), width, PSF_HALF)
        back_head, back_rest = square_band(line(c, 1), width, PSF_HALF)
        back_head_ref[c] = back_head
        back_rest_ref[c] = back_rest
        around = (
            jnp.dot(head, back_head, preferred_element_type=F32)
            + jnp.dot(rest, back_head, preferred_element_type=F32)
            + jnp.dot(head, back_rest, preferred_element_type=F32)
        )
        around_head_ref[c], around_rest_ref[c] = split(around)
        flag = flags_ref[c].astype(F32)
        adjoint = banded(line(c, 3), height) * flag
        adjoint = jnp.concatenate(halves(adjoint), axis=0)
        adj_ref[c] = wide_rows(adjoint[:, :reach])
        adjoint = adjoint * inside((height, LANES), 1)
        forward = banded(line(c, 2), reach)
        first, second = split(adjoint[:, :reach])
        head, rest = split(forward)
        normal = (
            jnp.dot(first, head, preferred_element_type=F32)
            + jnp.dot(second, head, preferred_element_type=F32)
            + jnp.dot(first, rest, preferred_element_type=F32)
        )
        mats_ref[c, :reach] = band
        mats_ref[c, reach:], far = by_side(normal)
        far_mats_ref[c] = far[half:]
        return carry

    lax.fori_loop(0, chans, body, 0, unroll=8)


def first_columns_kernel(odd_ref, own_ref, head_ref, rest_ref, near_ref, far_ref, band_ref, sum_ref):
    chans, height, width = own_ref.shape
    half = height // 2
    odd = odd_ref[0] == 1
    total = jnp.zeros((height, width), F32)
    for c in range(0, chans, GROUP):
        n = min(GROUP, chans - c)
        low, high = own_ref[c : c + n, :half], own_ref[c : c + n, half:]
        near, far = jnp.where(odd, low, high), jnp.where(odd, high, low)
        near_ref[c : c + n] = near
        far_ref[c : c + n] = far
        rows = jnp.concatenate([near, far], axis=1)
        band = times_columns(rows.reshape(n * height, width), head_ref[...], rest_ref[...])
        band = band.reshape(n, height, width)
        band_ref[c : c + n] = band
        total = total + jnp.sum(band * band, axis=0)
    sum_ref[...] = total


def first_gradient_kernel(
    part_ref, head_ref, rest_ref, dirty_ref, back_head_ref, back_rest_ref, adj_ref, data_ref, grad_ref
):
    chans = part_ref.shape[0]

    def body(c, carry):
        across = times_columns(dirty_ref[c], back_head_ref[c], back_rest_ref[c])
        data = jnp.dot(adj_ref[c], stacked(across), preferred_element_type=F32)
        data_ref[c] = data
        grad_ref[c] = times_columns(part_ref[c], head_ref[c], rest_ref[c]) - data
        return carry

    lax.fori_loop(0, chans, body, 0, unroll=4)


def gradient_kernel(part_ref, halo_ref, far_mats_ref, head_ref, rest_ref, data_ref, _, grad_ref):
    chans, height = part_ref.shape[:2]
    half = height // 2

    def body(c, carry):
        far = jnp.dot(far_mats_ref[c], stacked(halo_ref[c]), preferred_element_type=F32)
        part = jnp.concatenate([part_ref[c, :half], part_ref[c, half:] + far], axis=0)
        grad_ref[c] = times_columns(part, head_ref[c], rest_ref[c]) - data_ref[c]
        return carry

    lax.fori_loop(0, chans, body, 0, unroll=True)


def scaled(sums_refs, rows, radius):
    total = sums_refs[0][:rows]
    for ref in sums_refs[1:]:
        total = total + ref[:rows]
    length = jnp.sqrt(total)
    return radius / jnp.maximum(length, radius)


def radius_kernel(factor, *refs):
    *sums_refs, out_ref = refs
    skip = sums_refs[0].shape[0] - out_ref.shape[0]
    total = sums_refs[0][skip:]
    for ref in sums_refs[1:]:
        total = total + ref[skip:]
    out_ref[...] = factor / (jnp.sqrt(total) + WEIGHT_OFFSET)


def early_kernel(n_sums, *refs):
    sums_refs, refs = refs[:n_sums], refs[n_sums:]
    (
        radius_ref, moved_u_ref, moved1_ref, near_ref, far_ref, grad_ref, rows_ref, head_ref, rest_ref,
        dual_u_ref, dual1_ref, new_near_ref, half_far_ref,
    ) = refs
    chans, half, width = near_ref.shape
    height, free = 2 * half, moved_u_ref.shape[1]
    scale = scaled(sums_refs, free + height, radius_ref[: free + height])
    scale_u, scale1 = scale[:free], scale[free:]
    for c0 in range(0, chans, GROUP // 2):
        n = min(GROUP // 2, chans - c0)
        dual1 = moved1_ref[c0 : c0 + n] * scale1[None]
        dual1_ref[c0 : c0 + n] = dual1
        across = times_columns(dual1.reshape(n * height, width), head_ref[...], rest_ref[...])
        for c in range(c0, c0 + n):
            dual = moved_u_ref[c] * scale_u
            dual_u_ref[c] = dual
            down = jnp.dot(rows_ref[...], stacked(dual), preferred_element_type=F32)
            at = (c - c0) * height
            step = STEP_PRIMAL * (grad_ref[c] + (down + across[at : at + height]))
            new_near_ref[c] = jnp.maximum(near_ref[c] - step[:half], 0.0)
            half_far_ref[c] = far_ref[c] - step[half:]


def late_kernel(n_sums, odd_ref, *refs):
    sums_refs, refs = refs[:n_sums], refs[n_sums:]
    radius_ref, moved_ref, half_far_ref, rows_ref, dual_ref, new_ref, *rim_refs = refs
    chans, touched = moved_ref.shape[:2]
    odd = odd_ref[0] == 1
    scale = scaled(sums_refs, touched, radius_ref[radius_ref.shape[0] - touched :])

    def body(c, carry):
        dual = moved_ref[c] * scale
        dual_ref[c] = dual
        down = jnp.dot(rows_ref[...], stacked(dual), preferred_element_type=F32)
        new = jnp.maximum(half_far_ref[c] - STEP_PRIMAL * down, 0.0)
        new_ref[c] = new
        for ref in rim_refs:
            rim = ref.shape[1]
            ref[c] = jnp.where(odd, new[new.shape[0] - rim :], new[:rim])
        return carry

    lax.fori_loop(0, chans, body, 0, unroll=True)


def first_update_kernel(
    dual_u_ref, dual_t_ref, dual1_ref, near_ref, far_ref, grad_ref, rows_ref, rows_t_ref, head_ref, rest_ref,
    new_near_ref, new_far_ref,
):
    chans, half, width = near_ref.shape
    height = 2 * half
    for c0 in range(0, chans, GROUP // 2):
        n = min(GROUP // 2, chans - c0)
        across = times_columns(
            dual1_ref[c0 : c0 + n].reshape(n * height, width), head_ref[...], rest_ref[...]
        )
        for c in range(c0, c0 + n):
            down = jnp.dot(rows_ref[...], stacked(dual_u_ref[c]), preferred_element_type=F32)
            late = jnp.dot(rows_t_ref[...], stacked(dual_t_ref[c]), preferred_element_type=F32)
            at = (c - c0) * height
            step = grad_ref[c] + (down + across[at : at + height])
            new_near_ref[c] = jnp.maximum(near_ref[c] - STEP_PRIMAL * step[:half], 0.0)
            new_far_ref[c] = jnp.maximum(far_ref[c] - STEP_PRIMAL * (step[half:] + late), 0.0)


def final_early_kernel(n_sums, odd_ref, *refs):
    sums_refs, refs = refs[:n_sums], refs[n_sums:]
    radius_ref, moved_u_ref, moved1_ref, dual_u_ref, out_ref, plane, sem = refs
    chans, height, _ = moved1_ref.shape
    half, free = height // 2, moved_u_ref.shape[1]
    odd = odd_ref[0] == 1
    scale = scaled(sums_refs, free + height, radius_ref[: free + height])
    for c in range(chans):
        dual_u_ref[c] = moved_u_ref[c] * scale[:free]
        dual = moved1_ref[c] * scale[free:]
        near, far = dual[:half], dual[half:]
        plane[c, :half] = jnp.where(odd, near, far)
        plane[c, half:] = jnp.where(odd, far, near)
    copy = pltpu.make_async_copy(plane, out_ref.at[:, 1], sem)
    copy.start()
    copy.wait()


def final_late_kernel(n_sums, odd_ref, *refs):
    sums_refs, refs = refs[:n_sums], refs[n_sums:]
    radius_ref, moved_ref, dual_u_ref, _, out_ref, plane, sems = refs
    chans, height, _ = plane.shape
    touched, free = moved_ref.shape[1], dual_u_ref.shape[1]
    edge = (touched + free - height) // 2
    odd = odd_ref[0] == 1
    scale = scaled(sums_refs, touched, radius_ref[radius_ref.shape[0] - touched :])
    group = chans // sems.shape[0]
    copies = []
    for c in range(chans):
        dual = moved_ref[c] * scale
        above = jnp.concatenate([dual_u_ref[c, edge:], dual[: touched - edge]], axis=0)
        below = jnp.concatenate([dual[edge:], dual_u_ref[c, : free - edge]], axis=0)
        plane[c] = jnp.where(odd, above, below)
        if (c + 1) % group == 0:
            part = slice(c + 1 - group, c + 1)
            copies.append(
                pltpu.make_async_copy(plane.at[part], out_ref.at[part, 0], sems.at[len(copies)])
            )
            copies[-1].start()
    for copy in copies:
        copy.wait()


def publish_kernel(near_ref, far_ref, _, out_ref, sems):
    half = near_ref.shape[1]
    odd = lax.rem(lax.axis_index("facet"), 2)
    copies = [
        pltpu.make_async_copy(
            ref, out_ref.at[:, pl.ds(pl.multiple_of(low * half, 8), half)], sems.at[k]
        )
        for k, (ref, low) in enumerate(((near_ref, 1 - odd), (far_ref, odd)))
    ]
    for copy in copies:
        copy.start()
    for copy in copies:
        copy.wait()


def trade(values, across):
    n = lax.axis_size("facet")
    if across:
        pairs = [(i, ((i + 1) ^ 1) - 1) for i in range(n) if 0 <= ((i + 1) ^ 1) - 1 < n]
    else:
        pairs = [(i, i ^ 1) for i in range(n)]
    return lax.ppermute(values, "facet", pairs)


def peers(n, low):
    return sorted(range(1, min(4, n // low)), key=lambda k: -k.bit_count())


def gathered(sums):
    n = lax.axis_size("chan")
    if n & (n - 1):
        return [lax.psum(sums, "chan")]
    low = 1
    terms = [sums]
    while low < n:
        total = terms[0]
        for term in terms[1:]:
            total = total + term
        terms = [total]
        for k in peers(n, low):
            terms.append(lax.ppermute(total, "chan", [(i, i ^ (k * low)) for i in range(n)]))
        low *= min(4, n // low)
    return terms


def on_device(
    dirty_image, image_start, dual_start, psf_rows, psf_cols, wavelet_taps, channel_flags
):
    chans, height, width = image_start.shape
    total_chans = chans * lax.axis_size("chan")
    edge = max(PSF_HALF, WAV_HALF)
    reach, send = height + 2 * edge, 2 * edge
    passes = OUTER * INNER
    odd = (lax.axis_index("facet") % 2).astype(jnp.int32)[None]

    half, touched = height // 2, send
    free = reach - touched
    if half != send:
        raise ValueError("facet height")

    def rows(count):
        return (chans, count, width), F32

    own, side, wavy, late_rows = rows(height), rows(half), rows(free), rows(touched)
    late_sum = ((touched, width), F32)
    summed = ((reach + height, width), F32)
    square = ((width, width), BF16)
    squares = ((chans, width, width), BF16)

    first_sides = rows(2 * send)
    inputs = [pltpu.with_memory_space_constraint(x, pltpu.HBM) for x in (image_start, dual_start, dirty_image)]

    in_hbm = pl.BlockSpec(memory_space=pltpu.HBM)
    far, near = pl.pallas_call(
        pack_kernel,
        out_shape=[jax.ShapeDtypeStruct(*first_sides)] * 2,
        in_specs=[in_hbm] * 3,
        out_specs=[in_hbm] * 2,
        scratch_shapes=[pltpu.VMEM(*first_sides)] * 2 + [pltpu.SemaphoreType.DMA((6,))] * 2,
        compiler_params=PARAMS,
        name="pack",
    )(*inputs)
    far = trade(far, True)
    near = trade(near, False)

    def lines(cols, taps, half_c, half_r):
        def circle(taps, half):
            gap = jnp.zeros((taps.shape[0], LANES - 2 * half - 1), F32)
            return jnp.concatenate([taps[:, half:], gap, taps[:, :half]], axis=1)

        def ramp(taps, half):
            lead = jnp.zeros((taps.shape[0], edge - half), F32)
            gap = jnp.zeros((taps.shape[0], LANES - half - edge - 1), F32)
            return jnp.concatenate([lead, taps, gap], axis=1)

        return jnp.concatenate(
            [circle(cols[:, ::-1], half_c), circle(cols, half_c), ramp(taps, half_r), ramp(taps[:, ::-1], half_r)],
            axis=1,
        )

    table = jnp.concatenate(
        [
            lines(psf_cols, psf_rows, PSF_HALF, PSF_HALF),
            lines(wavelet_taps[1:2], wavelet_taps[0:1], WAV_HALF, WAV_HALF),
        ],
        axis=0,
    )
    (
        mats, far_band, far_mats, adjoint, wav_free, wav_touched, around_head, around_rest, back_head, back_rest,
        wav_head, wav_rest, wav_head_t, wav_rest_t,
    ) = call(
        matrices_kernel, (channel_flags, table[:, None]),
        (
            ((chans, reach + height, 3 * (height + send)), BF16), ((touched, 3 * send), BF16),
            ((chans, half, 3 * send), BF16), ((chans, height, 3 * reach), BF16),
            ((height, 3 * free), BF16), ((half, 3 * touched), BF16),
            squares, squares, squares, squares, square, square, square, square,
        ),
        1,
    )
    est_near, est_far, band1, sum1 = call(
        first_columns_kernel, (odd, image_start, wav_head, wav_rest),
        (side, side, own, ((height, width), F32)), 1,
    )
    band_u, band_t, part, dual_u, dual_t, dual1, dirty, weight_sums = call(
        first_rows_kernel,
        (odd, est_near, est_far, near, far, mats, far_band, far_mats, dual_start, dirty_image, sum1),
        (wavy, late_rows, own, wavy, late_rows, own, rows(reach), summed), 1,
    )
    data, grad = call(
        first_gradient_kernel,
        (part, around_head, around_rest, dirty, back_head, back_rest, adjoint), (own, own),
    )
    est_near, est_far = call(
        first_update_kernel,
        (dual_u, dual_t, dual1, est_near, est_far, grad, wav_free, wav_touched, wav_head_t, wav_rest_t),
        (side, side),
    )
    rim = est_far
    near = trade(est_near, False)
    for step in range(passes):
        last = step + 1 == passes
        far = trade(rim, True)
        weigh = step % INNER == 0
        moved_u, moved_t, moved1, sums, *bands = call(
            functools.partial(near_kernel, weigh, last),
            (est_near, est_far, near, mats, dual_u, dual_t, band_u, band_t, wav_head, wav_rest, dual1, band1)
            + ((weight_sums,) if weigh else ()),
            (wavy, late_rows, own, ((free + height + (summed[0][0] if weigh else 0), width), F32))
            + (() if last else (wavy, late_rows, own, own)),
        )
        if not last:
            band_u, band_t, part, band1 = bands
        early = gathered(sums)
        if weigh:
            radius = call(functools.partial(radius_kernel, RADIUS_SCALE * total_chans), tuple(early), (summed,))[0]
        moved_t, sums, *bands = call(
            functools.partial(far_kernel, send), (odd, far, far_band, band_t, moved_t),
            (late_rows, late_sum) + (() if last else (late_rows,)), 1,
        )
        if not last:
            band_t = bands[0]
        late = gathered(sums)
        if last:
            image_final = pl.pallas_call(
                publish_kernel,
                out_shape=jax.ShapeDtypeStruct(*own),
                in_specs=[VM, VM, pl.BlockSpec(memory_space=pl.ANY)],
                out_specs=pl.BlockSpec(memory_space=pltpu.HBM),
                scratch_shapes=[pltpu.SemaphoreType.DMA((2,))],
                compiler_params=PARAMS,
                name="publish",
            )(est_near, est_far, sums)
            result = jax.ShapeDtypeStruct((chans, 2, height, width), F32)
            dual_u, dual_final = pl.pallas_call(
                functools.partial(final_early_kernel, len(early)),
                out_shape=[jax.ShapeDtypeStruct(*wavy), result],
                in_specs=[SM] + [VM] * (len(early) + 3),
                out_specs=[VM, in_hbm],
                scratch_shapes=[pltpu.VMEM(*own), pltpu.SemaphoreType.DMA],
                compiler_params=PARAMS,
                name="final_early",
            )(odd, *early, radius, moved_u, moved1)
            dual_final = pl.pallas_call(
                functools.partial(final_late_kernel, len(late)),
                out_shape=result,
                in_specs=[SM] + [VM] * (len(late) + 3) + [in_hbm],
                out_specs=in_hbm,
                scratch_shapes=[pltpu.VMEM(*own), pltpu.SemaphoreType.DMA((4,))],
                input_output_aliases={len(late) + 4: 0},
                compiler_params=PARAMS,
                name="final_late",
            )(odd, *late, radius, moved_t, dual_u, dual_final)
            break
        grad = call(gradient_kernel, (part, far, far_mats, around_head, around_rest, data, sums), (own,))[0]
        dual_u, dual1, est_near, half_far = call(
            functools.partial(early_kernel, len(early)),
            (*early, radius, moved_u, moved1, est_near, est_far, grad, wav_free, wav_head_t, wav_rest_t),
            (wavy, own, side, side),
        )
        near = trade(est_near, False)
        if step % INNER == INNER - 1:
            weight_sums = call(squares_kernel, (band_u, band1, band_t), (summed,))[0]
        small = step + 2 == passes
        dual_t, est_far, *rims = call(
            functools.partial(late_kernel, len(late)),
            (odd, *late, radius, moved_t, half_far, wav_touched),
            (late_rows, side) + ((rows(WAV_HALF),) if small else ()), 1,
        )
        rim = rims[0] if small else est_far
    return (image_final, dual_final)


def solution(mesh):
    return jax.shard_map(
        on_device,
        mesh=mesh,
        in_specs=(
            P("chan", "facet", None),
            P("chan", "facet", None),
            P("chan", None, "facet", None),
            P("chan", None),
            P("chan", None),
            P(),
            P("chan"),
        ),
        out_specs=(P("chan", "facet", None), P("chan", None, "facet", None)),
        check_vma=False,
    )
```

```python
import functools

import jax
import jax.numpy as jnp
from jax import lax
from jax.experimental import pallas as pl
from jax.experimental.pallas import tpu as pltpu
from jax.sharding import PartitionSpec as P


PSF_HALF = 8
WAV_HALF = 8
OUTER = 2
INNER = 3

STEP_PRIMAL = 0.9
STEP_DUAL = 0.2
RADIUS_SCALE = 0.06
WEIGHT_OFFSET = 1.0


F32 = jnp.float32
BF16 = jnp.bfloat16
LANES = 128
GROUP = 8
VMEM_LIMIT = 24 * 1024 * 1024
PARAMS = pltpu.CompilerParams(vmem_limit_bytes=VMEM_LIMIT)


def split(values):
    head = values.astype(BF16)
    return head, (values - head.astype(F32)).astype(BF16)


def times_columns(values, head, rest):
    rows = values.shape[0]
    first, second = split(values)
    both = jnp.dot(jnp.concatenate([first, second], axis=0), head, preferred_element_type=F32)
    return both[:rows] + both[rows:] + jnp.dot(first, rest, preferred_element_type=F32)


def stacked(values):
    first, second = split(values)
    return jnp.concatenate([first, second, first], axis=0)


VM = pl.BlockSpec(memory_space=pltpu.VMEM)
SM = pl.BlockSpec(memory_space=pltpu.SMEM)


def call(kernel, ins, outs, scalars=0, scratch=()):
    return pl.pallas_call(
        kernel,
        out_shape=[jax.ShapeDtypeStruct(*shape) for shape in outs],
        in_specs=[SM] * scalars + [VM] * (len(ins) - scalars),
        out_specs=[VM] * len(outs),
        scratch_shapes=scratch,
        compiler_params=PARAMS,
    )(*ins)


def padded(odd, far, send):
    rows, width = far.shape
    if rows < send:
        blank = jnp.zeros((send - rows, width), F32)
        below, above = jnp.concatenate([far, blank], axis=0), jnp.concatenate([blank, far], axis=0)
        far = jnp.where(odd, below, above)
    return far


def near_kernel(
    weigh, last, near_ref, far_ref, halo_ref, mats_ref, dual_u_ref, dual_t_ref, old_u_ref, old_t_ref,
    head_ref, rest_ref, dual1_ref, old1_ref, *refs,
):
    refs = list(refs)
    extra_ref = refs.pop(0) if weigh else None
    moved_u_ref, moved_t_ref, moved1_ref, sums_ref = refs[:4]
    chans, half, width = near_ref.shape
    height, touched = 2 * half, moved_t_ref.shape[1]
    free = moved_u_ref.shape[1]

    def body(c, total):
        rows = jnp.concatenate([near_ref[c], far_ref[c], halo_ref[c]], axis=0)
        product = jnp.dot(mats_ref[c], stacked(rows), preferred_element_type=F32)
        band = product[:free]
        moved = dual_u_ref[c] + STEP_DUAL * (2.0 * band - old_u_ref[c])
        moved_u_ref[c] = moved
        band_t = product[free : free + touched]
        moved_t_ref[c] = dual_t_ref[c] + STEP_DUAL * (2.0 * band_t - old_t_ref[c])
        if not last:
            band_u_ref, band_t_ref, part_ref, _ = refs[4:]
            band_u_ref[c] = band
            band_t_ref[c] = band_t
            part_ref[c] = product[free + touched :]
        return total + moved * moved

    sums_ref[:free] = lax.fori_loop(0, chans, body, jnp.zeros((free, width), F32), unroll=True)
    total = jnp.zeros((height, width), F32)
    for c in range(0, chans, GROUP):
        n = min(GROUP, chans - c)
        rows = jnp.concatenate([near_ref[c : c + n], far_ref[c : c + n]], axis=1)
        band = times_columns(rows.reshape(n * height, width), head_ref[...], rest_ref[...])
        band = band.reshape(n, height, width)
        if not last:
            refs[7][c : c + n] = band
        moved = dual1_ref[c : c + n] + STEP_DUAL * (2.0 * band - old1_ref[c : c + n])
        moved1_ref[c : c + n] = moved
        total = total + jnp.sum(moved * moved, axis=0)
    sums_ref[free : free + height] = total
    if extra_ref is not None:
        sums_ref[free + height :] = extra_ref[...]


def far_kernel(send, odd_ref, far_ref, mats_ref, band_in_ref, moved_in_ref, moved_ref, sums_ref, *band_refs):
    chans, touched, width = moved_ref.shape
    odd = odd_ref[0] == 1

    def body(c, total):
        far = padded(odd, far_ref[c], send)
        product = jnp.dot(mats_ref[...], stacked(far), preferred_element_type=F32)
        for band_ref in band_refs:
            band_ref[c] = band_in_ref[c] + product
        moved = moved_in_ref[c] + (2.0 * STEP_DUAL) * product
        moved_ref[c] = moved
        return total + moved * moved

    sums_ref[...] = lax.fori_loop(0, chans, body, jnp.zeros((touched, width), F32), unroll=True)


def first_rows_kernel(
    near_ref, far_ref, halo_ref, far_halo_ref, mats_ref, far_band_ref, far_mats_ref, sum1_ref,
    band_u_ref, band_t_ref, part_ref, sums_ref,
):
    chans, half, width = near_ref.shape
    height, touched, free = 2 * half, band_t_ref.shape[1], band_u_ref.shape[1]
    send = far_mats_ref.shape[2] // 3

    def body(c, totals):
        rows = jnp.concatenate([near_ref[c], far_ref[c], halo_ref[c, :send]], axis=0)
        product = jnp.dot(mats_ref[c], stacked(rows), preferred_element_type=F32)
        far_rows = stacked(far_halo_ref[c])
        band_t = product[free : free + touched] + jnp.dot(
            far_band_ref[...], far_rows, preferred_element_type=F32
        )
        band = product[:free]
        band_u_ref[c] = band
        band_t_ref[c] = band_t
        at = free + touched + half
        part_ref[c, :half] = product[free + touched : at]
        part_ref[c, half:] = product[at:] + jnp.dot(far_mats_ref[c], far_rows, preferred_element_type=F32)
        return totals[0] + band * band, totals[1] + band_t * band_t

    zeros = jnp.zeros((free, width), F32), jnp.zeros((touched, width), F32)
    totals = lax.fori_loop(0, chans, body, zeros, unroll=True)
    sums_ref[:free] = totals[0]
    sums_ref[free : free + height] = sum1_ref[...]
    sums_ref[free + height :] = totals[1]


def first_data_kernel(
    odd_ref, halo_ref, far_halo_ref, start_ref, dirty_ref, adj_ref, back_head_ref, back_rest_ref,
    dual_u_ref, dual_t_ref, dual1_ref, data_ref,
):
    chans, height, _ = data_ref.shape
    half, touched, free = height // 2, dual_t_ref.shape[1], dual_u_ref.shape[1]
    edge = (touched + free - height) // 2
    send = halo_ref.shape[1] - 2 * edge
    odd = odd_ref[0] == 1

    def body(c, carry):
        near, far = halo_ref[c, send:], far_halo_ref[c]
        before, after = jnp.where(odd, near, far), jnp.where(odd, far, near)
        dual = jnp.concatenate([before[:edge], start_ref[c, 0], after[:edge]], axis=0)
        dual_u_ref[c] = jnp.where(odd, dual[:free], dual[touched:])
        dual_t_ref[c] = jnp.where(odd, dual[free:], dual[:touched])
        dual = start_ref[c, 1]
        dual1_ref[c, :half] = jnp.where(odd, dual[:half], dual[half:])
        dual1_ref[c, half:] = jnp.where(odd, dual[half:], dual[:half])
        dirty = jnp.concatenate([before[edge:], dirty_ref[c], after[edge:]], axis=0)
        part = jnp.dot(adj_ref[c], stacked(dirty), preferred_element_type=F32)
        data_ref[c] = times_columns(part, back_head_ref[c], back_rest_ref[c])
        return carry

    lax.fori_loop(0, chans, body, 0, unroll=True)


def squares_kernel(*refs):
    *band_refs, out_ref = refs
    at = 0
    for ref in band_refs:
        rows = ref.shape[1]
        out_ref[at : at + rows] = jnp.sum(ref[...] * ref[...], axis=0)
        at += rows


def pack_kernel(
    est_ref, dual_ref, dirty_ref, far_ref, later_ref, near_ref, far_rows, later_rows, near_rows, in_sems, out_sems
):
    height = est_ref.shape[1]
    send = far_ref.shape[1]
    edge = send // 2
    odd = lax.rem(lax.axis_index("facet"), 2)
    band_ref = dual_ref.at[:, 0]
    loads, stores = [], []
    for out_ref, held, low, at, ref, rows in (
        (far_ref, far_rows, odd, 0, est_ref, send),
        (later_ref, later_rows, odd, 0, band_ref, edge),
        (later_ref, later_rows, odd, edge, dirty_ref, edge),
        (near_ref, near_rows, 1 - odd, 0, est_ref, send),
        (near_ref, near_rows, 1 - odd, send, band_ref, edge),
        (near_ref, near_rows, 1 - odd, send + edge, dirty_ref, edge),
    ):
        start = pl.multiple_of(low * (height - rows), 8)
        k = len(loads)
        piece = (slice(None), slice(at, at + rows))
        loads.append(pltpu.make_async_copy(ref.at[:, pl.ds(start, rows)], held.at[piece], in_sems.at[k]))
        stores.append(pltpu.make_async_copy(held.at[piece], out_ref.at[piece], out_sems.at[k]))
    for load in loads:
        load.start()
    for load, store in zip(loads, stores):
        load.wait()
        store.start()
    for store in stores:
        store.wait()


def banded(line, rows):
    return pltpu.roll(
        jnp.broadcast_to(line, (rows, LANES)), 0, 1, stride=1, stride_axis=0
    )


def square_band(line, width, half):
    around = banded(line, LANES)
    offset = lax.broadcasted_iota(jnp.int32, (LANES, LANES), 1) - lax.broadcasted_iota(
        jnp.int32, (LANES, LANES), 0
    )
    parts = []
    for piece in split(around):
        piece = piece.astype(F32)
        middle = jnp.where(jnp.abs(offset) <= half, piece, 0.0).astype(BF16)
        right = jnp.where(offset <= half - LANES, piece, 0.0).astype(BF16)
        left = jnp.where(offset >= LANES - half, piece, 0.0).astype(BF16)
        blank = jnp.zeros((LANES, LANES), BF16)
        tiles = width // LANES
        kinds = {0: middle, 1: right, -1: left}
        parts.append(
            jnp.concatenate(
                [
                    jnp.concatenate([kinds.get(j - i, blank) for j in range(tiles)], axis=1)
                    for i in range(tiles)
                ],
                axis=0,
            )
        )
    return parts


def matrices_kernel(
    flags_ref, cols_ref, rows_ref, wav_ref, mats_ref, far_band_ref, far_mats_ref, adj_ref, wav_free_ref, wav_touched_ref,
    around_head_ref, around_rest_ref, back_head_ref, back_rest_ref,
    wav_head_ref, wav_rest_ref, wav_head_t_ref, wav_rest_t_ref, lines_ref,
):
    chans, width = around_head_ref.shape[:2]
    send = far_mats_ref.shape[2] // 3
    height, reach = adj_ref.shape[1], adj_ref.shape[2] // 3
    half, touched = height // 2, far_band_ref.shape[0]
    free = reach - touched
    edge = (reach - height) // 2
    facet, facets = lax.axis_index("facet"), lax.axis_size("facet")
    odd = lax.rem(facet, 2) == 1

    def inside(shape, dim):
        at = lax.broadcasted_iota(jnp.int32, shape, dim)
        low = jnp.where(facet > 0, 0, edge)
        high = jnp.where(facet < facets - 1, reach, reach - edge)
        return jnp.where((at >= low) & (at < high), 1.0, 0.0)

    def placed(taps, first, back):
        count = taps.shape[1]
        lane = lax.broadcasted_iota(jnp.int32, (count, LANES), 1)
        tap = lax.broadcasted_iota(jnp.int32, (count, LANES), 0)
        at = jnp.where(lane >= first, lane - first, lane - first + LANES) if first >= 0 else jnp.where(
            lane - first < LANES, lane - first, lane - first - LANES
        )
        pick = jnp.where((count - 1 - at if back else at) == tap, 1.0, 0.0)
        return jnp.dot(taps, pick, precision=lax.Precision.HIGHEST, preferred_element_type=F32)

    def put(at, cols, rows, half_c, half_r):
        lines = jnp.concatenate(
            [
                placed(cols, -half_c, True), placed(cols, -half_c, False),
                placed(rows, edge - half_r, False), placed(rows, edge - half_r, True),
            ],
            axis=1,
        )
        for c in range(lines.shape[0]):
            lines_ref[at + c] = lines[c : c + 1]

    put(0, cols_ref[...], rows_ref[...], PSF_HALF, PSF_HALF)
    put(chans, wav_ref[1:2], wav_ref[0:1], WAV_HALF, WAV_HALF)

    def line(c, k):
        return lines_ref[c, :, k * LANES : (k + 1) * LANES]

    def wide_rows(matrix):
        first, second = split(matrix)
        first, second = first.astype(F32), second.astype(F32)
        return jnp.concatenate([first, first, second], axis=1).astype(BF16)

    wav_head_ref[...], wav_rest_ref[...] = square_band(line(chans, 0), width, WAV_HALF)
    wav_head_t_ref[...], wav_rest_t_ref[...] = square_band(line(chans, 1), width, WAV_HALF)

    def halves(matrix):
        low, high = matrix[:half], matrix[half:]
        return jnp.where(odd, low, high), jnp.where(odd, high, low)

    def reached(matrix):
        return jnp.where(odd, matrix[:free], matrix[touched:]), jnp.where(odd, matrix[free:], matrix[:touched])

    near, far = halves(banded(line(chans, 3), height)[:, :reach])
    wav_free_ref[...] = wide_rows(
        jnp.concatenate([jnp.where(odd, x[:, :free], x[:, touched:]) for x in (near, far)], axis=0)
    )
    wav_touched_ref[...] = wide_rows(jnp.where(odd, far[:, free:], far[:, :touched]))

    def by_side(matrix):
        low, high = matrix[:, :send], matrix[:, send + height : 2 * send + height]
        first, second = matrix[:, send : send + half], matrix[:, send + half : send + height]
        own = jnp.where(odd, first, second), jnp.where(odd, second, first)
        near, far = jnp.where(odd, low, high), jnp.where(odd, high, low)
        return wide_rows(jnp.concatenate([*own, near], axis=1)), wide_rows(far)

    band = banded(line(chans, 2), reach) * inside((reach, LANES), 0)
    band, far_band = by_side(jnp.concatenate(reached(band), axis=0))
    far_band_ref[...] = far_band[free:]

    def body(c, carry):
        head, rest = square_band(line(c, 0), width, PSF_HALF)
        back_head, back_rest = square_band(line(c, 1), width, PSF_HALF)
        back_head_ref[c] = back_head
        back_rest_ref[c] = back_rest
        around = (
            jnp.dot(head, back_head, preferred_element_type=F32)
            + jnp.dot(rest, back_head, preferred_element_type=F32)
            + jnp.dot(head, back_rest, preferred_element_type=F32)
        )
        around_head_ref[c], around_rest_ref[c] = split(around)
        flag = flags_ref[c].astype(F32)
        adjoint = banded(line(c, 3), height) * flag
        adjoint = jnp.concatenate(halves(adjoint), axis=0)
        adj_ref[c] = wide_rows(adjoint[:, :reach])
        adjoint = adjoint * inside((height, LANES), 1)
        forward = banded(line(c, 2), reach)
        first, second = split(adjoint[:, :reach])
        head, rest = split(forward)
        normal = (
            jnp.dot(first, head, preferred_element_type=F32)
            + jnp.dot(second, head, preferred_element_type=F32)
            + jnp.dot(first, rest, preferred_element_type=F32)
        )
        mats_ref[c, :reach] = band
        mats_ref[c, reach:], far = by_side(normal)
        far_mats_ref[c] = far[half:]
        return carry

    lax.fori_loop(0, chans, body, 0, unroll=8)


def first_columns_kernel(odd_ref, own_ref, head_ref, rest_ref, near_ref, far_ref, band_ref, sum_ref):
    chans, height, width = own_ref.shape
    half = height // 2
    odd = odd_ref[0] == 1
    total = jnp.zeros((height, width), F32)
    for c in range(0, chans, GROUP):
        n = min(GROUP, chans - c)
        low, high = own_ref[c : c + n, :half], own_ref[c : c + n, half:]
        near, far = jnp.where(odd, low, high), jnp.where(odd, high, low)
        near_ref[c : c + n] = near
        far_ref[c : c + n] = far
        rows = jnp.concatenate([near, far], axis=1)
        band = times_columns(rows.reshape(n * height, width), head_ref[...], rest_ref[...])
        band = band.reshape(n, height, width)
        band_ref[c : c + n] = band
        total = total + jnp.sum(band * band, axis=0)
    sum_ref[...] = total


def first_gradient_kernel(part_ref, head_ref, rest_ref, grad_ref):
    def body(c, carry):
        grad_ref[c] = times_columns(part_ref[c], head_ref[c], rest_ref[c])
        return carry

    lax.fori_loop(0, part_ref.shape[0], body, 0, unroll=True)


def gradient_kernel(part_ref, halo_ref, far_mats_ref, head_ref, rest_ref, data_ref, _, grad_ref):
    chans, height = part_ref.shape[:2]
    half = height // 2

    def body(c, carry):
        far = jnp.dot(far_mats_ref[c], stacked(halo_ref[c]), preferred_element_type=F32)
        part = jnp.concatenate([part_ref[c, :half], part_ref[c, half:] + far], axis=0)
        grad_ref[c] = times_columns(part, head_ref[c], rest_ref[c]) - data_ref[c]
        return carry

    lax.fori_loop(0, chans, body, 0, unroll=True)


def scaled(sums_refs, rows, radius):
    total = sums_refs[0][:rows]
    for ref in sums_refs[1:]:
        total = total + ref[:rows]
    length = jnp.sqrt(total)
    return radius / jnp.maximum(length, radius)


def radius_kernel(factor, *refs):
    *sums_refs, out_ref = refs
    skip = sums_refs[0].shape[0] - out_ref.shape[0]
    total = sums_refs[0][skip:]
    for ref in sums_refs[1:]:
        total = total + ref[skip:]
    out_ref[...] = factor / (jnp.sqrt(total) + WEIGHT_OFFSET)


def early_kernel(n_sums, *refs):
    sums_refs, refs = refs[:n_sums], refs[n_sums:]
    (
        radius_ref, moved_u_ref, moved1_ref, near_ref, far_ref, grad_ref, rows_ref, head_ref, rest_ref,
        dual_u_ref, dual1_ref, new_near_ref, half_far_ref,
    ) = refs
    chans, half, width = near_ref.shape
    height, free = 2 * half, moved_u_ref.shape[1]
    scale = scaled(sums_refs, free + height, radius_ref[: free + height])
    scale_u, scale1 = scale[:free], scale[free:]
    for c0 in range(0, chans, GROUP // 2):
        n = min(GROUP // 2, chans - c0)
        dual1 = moved1_ref[c0 : c0 + n] * scale1[None]
        dual1_ref[c0 : c0 + n] = dual1
        across = times_columns(dual1.reshape(n * height, width), head_ref[...], rest_ref[...])
        for c in range(c0, c0 + n):
            dual = moved_u_ref[c] * scale_u
            dual_u_ref[c] = dual
            down = jnp.dot(rows_ref[...], stacked(dual), preferred_element_type=F32)
            at = (c - c0) * height
            step = STEP_PRIMAL * (grad_ref[c] + (down + across[at : at + height]))
            new_near_ref[c] = jnp.maximum(near_ref[c] - step[:half], 0.0)
            half_far_ref[c] = far_ref[c] - step[half:]


def late_kernel(n_sums, odd_ref, *refs):
    sums_refs, refs = refs[:n_sums], refs[n_sums:]
    radius_ref, moved_ref, half_far_ref, rows_ref, dual_ref, new_ref, *rim_refs = refs
    chans, touched = moved_ref.shape[:2]
    odd = odd_ref[0] == 1
    scale = scaled(sums_refs, touched, radius_ref[radius_ref.shape[0] - touched :])

    def body(c, carry):
        dual = moved_ref[c] * scale
        dual_ref[c] = dual
        down = jnp.dot(rows_ref[...], stacked(dual), preferred_element_type=F32)
        new = jnp.maximum(half_far_ref[c] - STEP_PRIMAL * down, 0.0)
        new_ref[c] = new
        for ref in rim_refs:
            rim = ref.shape[1]
            ref[c] = jnp.where(odd, new[new.shape[0] - rim :], new[:rim])
        return carry

    lax.fori_loop(0, chans, body, 0, unroll=True)


def first_update_kernel(
    dual_u_ref, dual_t_ref, dual1_ref, near_ref, far_ref, grad_ref, data_ref, rows_ref, rows_t_ref, head_ref,
    rest_ref, new_near_ref, new_far_ref,
):
    chans, half, width = near_ref.shape
    height = 2 * half
    for c0 in range(0, chans, GROUP // 2):
        n = min(GROUP // 2, chans - c0)
        across = times_columns(
            dual1_ref[c0 : c0 + n].reshape(n * height, width), head_ref[...], rest_ref[...]
        )
        for c in range(c0, c0 + n):
            down = jnp.dot(rows_ref[...], stacked(dual_u_ref[c]), preferred_element_type=F32)
            late = jnp.dot(rows_t_ref[...], stacked(dual_t_ref[c]), preferred_element_type=F32)
            at = (c - c0) * height
            step = (grad_ref[c] - data_ref[c]) + (down + across[at : at + height])
            new_near_ref[c] = jnp.maximum(near_ref[c] - STEP_PRIMAL * step[:half], 0.0)
            new_far_ref[c] = jnp.maximum(far_ref[c] - STEP_PRIMAL * (step[half:] + late), 0.0)


def final_early_kernel(n_sums, odd_ref, *refs):
    sums_refs, refs = refs[:n_sums], refs[n_sums:]
    radius_ref, moved_u_ref, moved1_ref, out_ref, across, down, sems = refs
    chans, height, _ = moved1_ref.shape
    half, free, kept = height // 2, moved_u_ref.shape[1], down.shape[1]
    odd = odd_ref[0] == 1
    scale = scaled(sums_refs, free + height, radius_ref[: free + height])
    start = pl.multiple_of((1 - lax.rem(lax.axis_index("facet"), 2)) * (height - kept), 8)
    low, high = out_ref.at[:, 1], out_ref.at[:, 0, pl.ds(start, kept)]
    for c in range(chans):
        dual = moved1_ref[c] * scale[free:]
        near, far = dual[:half], dual[half:]
        across[c, :half] = jnp.where(odd, near, far)
        across[c, half:] = jnp.where(odd, far, near)
    copies = [pltpu.make_async_copy(across, low, sems.at[0]), pltpu.make_async_copy(down, high, sems.at[1])]
    copies[0].start()
    for c in range(chans):
        dual = moved_u_ref[c] * scale[:free]
        down[c] = jnp.where(odd, dual[free - kept :], dual[:kept])
    copies[1].start()
    for copy in copies:
        copy.wait()


def final_late_kernel(n_sums, odd_ref, *refs):
    sums_refs, refs = refs[:n_sums], refs[n_sums:]
    radius_ref, moved_ref, _, out_ref, down, sem = refs
    chans, height, width = out_ref.shape[0], *out_ref.shape[2:]
    touched, rest = moved_ref.shape[1], down.shape[1]
    odd = odd_ref[0] == 1
    scale = scaled(sums_refs, touched, radius_ref[radius_ref.shape[0] - touched :])
    for c in range(chans):
        dual = moved_ref[c] * scale
        down[c] = jnp.where(odd, dual[:rest], dual[touched - rest :])
    start = pl.multiple_of(lax.rem(lax.axis_index("facet"), 2) * (height - rest), 8)
    copy = pltpu.make_async_copy(down, out_ref.at[:, 0, pl.ds(start, rest)], sem)
    copy.start()
    copy.wait()


def publish_kernel(near_ref, far_ref, _, out_ref, sems):
    half = near_ref.shape[1]
    odd = lax.rem(lax.axis_index("facet"), 2)
    copies = [
        pltpu.make_async_copy(
            ref, out_ref.at[:, pl.ds(pl.multiple_of(low * half, 8), half)], sems.at[k]
        )
        for k, (ref, low) in enumerate(((near_ref, 1 - odd), (far_ref, odd)))
    ]
    for copy in copies:
        copy.start()
    for copy in copies:
        copy.wait()


def trade(values, across):
    n = lax.axis_size("facet")
    if across:
        pairs = [(i, ((i + 1) ^ 1) - 1) for i in range(n) if 0 <= ((i + 1) ^ 1) - 1 < n]
    else:
        pairs = [(i, i ^ 1) for i in range(n)]
    return lax.ppermute(values, "facet", pairs)


def peers(n, low):
    return sorted(range(1, min(4, n // low)), key=lambda k: -k.bit_count())


def gathered(sums):
    n = lax.axis_size("chan")
    if n & (n - 1):
        return [lax.psum(sums, "chan")]
    low = 1
    terms = [sums]
    while low < n:
        total = terms[0]
        for term in terms[1:]:
            total = total + term
        terms = [total]
        for k in peers(n, low):
            terms.append(lax.ppermute(total, "chan", [(i, i ^ (k * low)) for i in range(n)]))
        low *= min(4, n // low)
    return terms


def on_device(
    dirty_image, image_start, dual_start, psf_rows, psf_cols, wavelet_taps, channel_flags
):
    chans, height, width = image_start.shape
    total_chans = chans * lax.axis_size("chan")
    edge = max(PSF_HALF, WAV_HALF)
    reach, send = height + 2 * edge, 2 * edge
    passes = OUTER * INNER
    odd = (lax.axis_index("facet") % 2).astype(jnp.int32)[None]

    half, touched = height // 2, send
    free = reach - touched
    if half != send:
        raise ValueError("facet height")

    def rows(count):
        return (chans, count, width), F32

    own, side, wavy, late_rows = rows(height), rows(half), rows(free), rows(touched)
    late_sum = ((touched, width), F32)
    summed = ((reach + height, width), F32)
    square = ((width, width), BF16)
    squares = ((chans, width, width), BF16)

    inputs = [pltpu.with_memory_space_constraint(x, pltpu.HBM) for x in (image_start, dual_start, dirty_image)]

    in_hbm = pl.BlockSpec(memory_space=pltpu.HBM)
    packs = (rows(send), rows(2 * edge), rows(send + 2 * edge))
    far, later, near = pl.pallas_call(
        pack_kernel,
        out_shape=[jax.ShapeDtypeStruct(*pack) for pack in packs],
        in_specs=[in_hbm] * 3,
        out_specs=[in_hbm] * 3,
        scratch_shapes=[pltpu.VMEM(*pack) for pack in packs] + [pltpu.SemaphoreType.DMA((6,))] * 2,
        compiler_params=PARAMS,
        name="pack",
    )(*inputs)
    far = trade(far, True)
    later = trade(later, True)

    (
        mats, far_band, far_mats, adjoint, wav_free, wav_touched, around_head, around_rest, back_head, back_rest,
        wav_head, wav_rest, wav_head_t, wav_rest_t,
    ) = call(
        matrices_kernel, (channel_flags, psf_cols, psf_rows, wavelet_taps),
        (
            ((chans, reach + height, 3 * (height + send)), BF16), ((touched, 3 * send), BF16),
            ((chans, half, 3 * send), BF16), ((chans, height, 3 * reach), BF16),
            ((height, 3 * free), BF16), ((half, 3 * touched), BF16),
            squares, squares, squares, squares, square, square, square, square,
        ),
        1, scratch=(pltpu.VMEM((chans + 1, 1, 4 * LANES), F32),),
    )
    near = trade(near, False)
    est_near, est_far, band1, sum1 = call(
        first_columns_kernel, (odd, image_start, wav_head, wav_rest),
        (side, side, own, ((height, width), F32)), 1,
    )
    band_u, band_t, part, weight_sums = call(
        first_rows_kernel, (est_near, est_far, near, far, mats, far_band, far_mats, sum1),
        (wavy, late_rows, own, summed),
    )
    grad = call(first_gradient_kernel, (part, around_head, around_rest), (own,))[0]
    dual_u, dual_t, dual1, data = call(
        first_data_kernel, (odd, near, later, dual_start, dirty_image, adjoint, back_head, back_rest),
        (wavy, late_rows, own, own), 1,
    )
    est_near, est_far = call(
        first_update_kernel,
        (dual_u, dual_t, dual1, est_near, est_far, grad, data, wav_free, wav_touched, wav_head_t, wav_rest_t),
        (side, side),
    )
    rim = est_far
    near = trade(est_near, False)
    for step in range(passes):
        last = step + 1 == passes
        far = trade(rim, True)
        weigh = step % INNER == 0
        moved_u, moved_t, moved1, sums, *bands = call(
            functools.partial(near_kernel, weigh, last),
            (est_near, est_far, near, mats, dual_u, dual_t, band_u, band_t, wav_head, wav_rest, dual1, band1)
            + ((weight_sums,) if weigh else ()),
            (wavy, late_rows, own, ((free + height + (summed[0][0] if weigh else 0), width), F32))
            + (() if last else (wavy, late_rows, own, own)),
        )
        if not last:
            band_u, band_t, part, band1 = bands
        early = gathered(sums)
        if weigh:
            radius = call(functools.partial(radius_kernel, RADIUS_SCALE * total_chans), tuple(early), (summed,))[0]
        moved_t, sums, *bands = call(
            functools.partial(far_kernel, send), (odd, far, far_band, band_t, moved_t),
            (late_rows, late_sum) + (() if last else (late_rows,)), 1,
        )
        if not last:
            band_t = bands[0]
        late = gathered(sums)
        if last:
            image_final = pl.pallas_call(
                publish_kernel,
                out_shape=jax.ShapeDtypeStruct(*own),
                in_specs=[VM, VM, pl.BlockSpec(memory_space=pl.ANY)],
                out_specs=pl.BlockSpec(memory_space=pltpu.HBM),
                scratch_shapes=[pltpu.SemaphoreType.DMA((2,))],
                compiler_params=PARAMS,
                name="publish",
            )(est_near, est_far, sums)
            result = jax.ShapeDtypeStruct((chans, 2, height, width), F32)
            rest = touched - edge
            dual_final = pl.pallas_call(
                functools.partial(final_early_kernel, len(early)),
                out_shape=result,
                in_specs=[SM] + [VM] * (len(early) + 3),
                out_specs=in_hbm,
                scratch_shapes=[
                    pltpu.VMEM(*own), pltpu.VMEM(*rows(height - rest)), pltpu.SemaphoreType.DMA((2,))
                ],
                compiler_params=PARAMS,
                name="final_early",
            )(odd, *early, radius, moved_u, moved1)
            dual_final = pl.pallas_call(
                functools.partial(final_late_kernel, len(late)),
                out_shape=result,
                in_specs=[SM] + [VM] * (len(late) + 2) + [in_hbm],
                out_specs=in_hbm,
                scratch_shapes=[pltpu.VMEM(*rows(rest)), pltpu.SemaphoreType.DMA],
                input_output_aliases={len(late) + 3: 0},
                compiler_params=PARAMS,
                name="final_late",
            )(odd, *late, radius, moved_t, dual_final)
            break
        grad = call(gradient_kernel, (part, far, far_mats, around_head, around_rest, data, sums), (own,))[0]
        dual_u, dual1, est_near, half_far = call(
            functools.partial(early_kernel, len(early)),
            (*early, radius, moved_u, moved1, est_near, est_far, grad, wav_free, wav_head_t, wav_rest_t),
            (wavy, own, side, side),
        )
        near = trade(est_near, False)
        if step % INNER == INNER - 1:
            weight_sums = call(squares_kernel, (band_u, band1, band_t), (summed,))[0]
        small = step + 2 == passes
        dual_t, est_far, *rims = call(
            functools.partial(late_kernel, len(late)),
            (odd, *late, radius, moved_t, half_far, wav_touched),
            (late_rows, side) + ((rows(WAV_HALF),) if small else ()), 1,
        )
        rim = rims[0] if small else est_far
    return (image_final, dual_final)


def solution(mesh):
    return jax.shard_map(
        on_device,
        mesh=mesh,
        in_specs=(
            P("chan", "facet", None),
            P("chan", "facet", None),
            P("chan", None, "facet", None),
            P("chan", None),
            P("chan", None),
            P(),
            P("chan"),
        ),
        out_specs=(P("chan", "facet", None), P("chan", None, "facet", None)),
        check_vma=False,
    )
```

```python
import functools

import jax
import jax.numpy as jnp
from jax import lax
from jax.experimental import pallas as pl
from jax.experimental.pallas import tpu as pltpu
from jax.sharding import PartitionSpec as P


PSF_HALF = 8
WAV_HALF = 8
OUTER = 2
INNER = 3

STEP_PRIMAL = 0.9
STEP_DUAL = 0.2
RADIUS_SCALE = 0.06
WEIGHT_OFFSET = 1.0


F32 = jnp.float32
BF16 = jnp.bfloat16
LANES = 128
GROUP = 8
VMEM_LIMIT = 24 * 1024 * 1024
PARAMS = pltpu.CompilerParams(vmem_limit_bytes=VMEM_LIMIT)


def split(values):
    head = values.astype(BF16)
    return head, (values - head.astype(F32)).astype(BF16)


def times_columns(values, head, rest):
    rows = values.shape[0]
    first, second = split(values)
    both = jnp.dot(jnp.concatenate([first, second], axis=0), head, preferred_element_type=F32)
    return both[:rows] + both[rows:] + jnp.dot(first, rest, preferred_element_type=F32)


def stacked(values):
    first, second = split(values)
    return jnp.concatenate([first, second, first], axis=0)


VM = pl.BlockSpec(memory_space=pltpu.VMEM)
SM = pl.BlockSpec(memory_space=pltpu.SMEM)


def call(kernel, ins, outs, scalars=0, scratch=()):
    return pl.pallas_call(
        kernel,
        out_shape=[jax.ShapeDtypeStruct(*shape) for shape in outs],
        in_specs=[SM] * scalars + [VM] * (len(ins) - scalars),
        out_specs=[VM] * len(outs),
        scratch_shapes=scratch,
        compiler_params=PARAMS,
    )(*ins)


def padded(odd, far, send):
    rows, width = far.shape
    if rows < send:
        blank = jnp.zeros((send - rows, width), F32)
        below, above = jnp.concatenate([far, blank], axis=0), jnp.concatenate([blank, far], axis=0)
        far = jnp.where(odd, below, above)
    return far


def near_kernel(
    weigh, last, near_ref, far_ref, halo_ref, mats_ref, dual_u_ref, dual_t_ref, old_u_ref, old_t_ref,
    head_ref, rest_ref, dual1_ref, old1_ref, *refs,
):
    refs = list(refs)
    extra_ref = refs.pop(0) if weigh else None
    moved_u_ref, moved_t_ref, moved1_ref, sums_ref = refs[:4]
    chans, half, width = near_ref.shape
    height, touched = 2 * half, moved_t_ref.shape[1]
    free = moved_u_ref.shape[1]

    def body(c, total):
        rows = jnp.concatenate([near_ref[c], far_ref[c], halo_ref[c]], axis=0)
        product = jnp.dot(mats_ref[c], stacked(rows), preferred_element_type=F32)
        band = product[:free]
        moved = dual_u_ref[c] + STEP_DUAL * (2.0 * band - old_u_ref[c])
        moved_u_ref[c] = moved
        band_t = product[free : free + touched]
        moved_t_ref[c] = dual_t_ref[c] + STEP_DUAL * (2.0 * band_t - old_t_ref[c])
        if not last:
            band_u_ref, band_t_ref, part_ref, _ = refs[4:]
            band_u_ref[c] = band
            band_t_ref[c] = band_t
            part_ref[c] = product[free + touched :]
        return total + moved * moved

    sums_ref[:free] = lax.fori_loop(0, chans, body, jnp.zeros((free, width), F32), unroll=True)
    total = jnp.zeros((height, width), F32)
    for c in range(0, chans, GROUP):
        n = min(GROUP, chans - c)
        rows = jnp.concatenate([near_ref[c : c + n], far_ref[c : c + n]], axis=1)
        band = times_columns(rows.reshape(n * height, width), head_ref[...], rest_ref[...])
        band = band.reshape(n, height, width)
        if not last:
            refs[7][c : c + n] = band
        moved = dual1_ref[c : c + n] + STEP_DUAL * (2.0 * band - old1_ref[c : c + n])
        moved1_ref[c : c + n] = moved
        total = total + jnp.sum(moved * moved, axis=0)
    sums_ref[free : free + height] = total
    if extra_ref is not None:
        sums_ref[free + height :] = extra_ref[...]


def far_kernel(send, odd_ref, far_ref, mats_ref, band_in_ref, moved_in_ref, moved_ref, sums_ref, *band_refs):
    chans, touched, width = moved_ref.shape
    odd = odd_ref[0] == 1

    def body(c, total):
        far = padded(odd, far_ref[c], send)
        product = jnp.dot(mats_ref[...], stacked(far), preferred_element_type=F32)
        for band_ref in band_refs:
            band_ref[c] = band_in_ref[c] + product
        moved = moved_in_ref[c] + (2.0 * STEP_DUAL) * product
        moved_ref[c] = moved
        return total + moved * moved

    sums_ref[...] = lax.fori_loop(0, chans, body, jnp.zeros((touched, width), F32), unroll=True)


def first_rows_kernel(
    near_ref, far_ref, halo_ref, far_halo_ref, mats_ref, far_band_ref, far_mats_ref, sum1_ref,
    band_u_ref, band_t_ref, part_ref, sums_ref,
):
    chans, half, width = near_ref.shape
    height, touched, free = 2 * half, band_t_ref.shape[1], band_u_ref.shape[1]
    send = far_mats_ref.shape[2] // 3

    def body(c, totals):
        rows = jnp.concatenate([near_ref[c], far_ref[c], halo_ref[c, :send]], axis=0)
        product = jnp.dot(mats_ref[c], stacked(rows), preferred_element_type=F32)
        far_rows = stacked(far_halo_ref[c])
        band_t = product[free : free + touched] + jnp.dot(
            far_band_ref[...], far_rows, preferred_element_type=F32
        )
        band = product[:free]
        band_u_ref[c] = band
        band_t_ref[c] = band_t
        at = free + touched + half
        part_ref[c, :half] = product[free + touched : at]
        part_ref[c, half:] = product[at:] + jnp.dot(far_mats_ref[c], far_rows, preferred_element_type=F32)
        return totals[0] + band * band, totals[1] + band_t * band_t

    zeros = jnp.zeros((free, width), F32), jnp.zeros((touched, width), F32)
    totals = lax.fori_loop(0, chans, body, zeros, unroll=True)
    sums_ref[:free] = totals[0]
    sums_ref[free : free + height] = sum1_ref[...]
    sums_ref[free + height :] = totals[1]


def first_data_kernel(
    odd_ref, halo_ref, far_halo_ref, start_ref, dirty_ref, adj_ref, back_head_ref, back_rest_ref,
    dual_u_ref, dual_t_ref, dual1_ref, data_ref, part_ref,
):
    chans, height, _ = data_ref.shape
    half, touched, free = height // 2, dual_t_ref.shape[1], dual_u_ref.shape[1]
    edge = (touched + free - height) // 2
    send = halo_ref.shape[1] - 2 * edge
    odd = odd_ref[0] == 1

    def body(c, carry):
        near, far = halo_ref[c, send:], far_halo_ref[c]
        before, after = jnp.where(odd, near, far), jnp.where(odd, far, near)
        dual = jnp.concatenate([before[:edge], start_ref[c, 0], after[:edge]], axis=0)
        dual_u_ref[c] = jnp.where(odd, dual[:free], dual[touched:])
        dual_t_ref[c] = jnp.where(odd, dual[free:], dual[:touched])
        dual = start_ref[c, 1]
        dual1_ref[c, :half] = jnp.where(odd, dual[:half], dual[half:])
        dual1_ref[c, half:] = jnp.where(odd, dual[half:], dual[:half])
        dirty = jnp.concatenate([before[edge:], dirty_ref[c], after[edge:]], axis=0)
        part_ref[c] = jnp.dot(adj_ref[c], stacked(dirty), preferred_element_type=F32)
        return carry

    def columns(c, carry):
        data_ref[c] = times_columns(part_ref[c], back_head_ref[c], back_rest_ref[c])
        return carry

    lax.fori_loop(0, chans, body, 0, unroll=True)
    lax.fori_loop(0, chans, columns, 0, unroll=True)


def squares_kernel(*refs):
    *band_refs, out_ref = refs
    at = 0
    for ref in band_refs:
        rows = ref.shape[1]
        out_ref[at : at + rows] = jnp.sum(ref[...] * ref[...], axis=0)
        at += rows


def pack_kernel(
    est_ref, dual_ref, dirty_ref, far_ref, later_ref, near_ref, far_rows, later_rows, near_rows, in_sems, out_sems
):
    height = est_ref.shape[1]
    send = far_ref.shape[1]
    edge = send // 2
    odd = lax.rem(lax.axis_index("facet"), 2)
    band_ref = dual_ref.at[:, 0]
    loads, stores = [], []
    for out_ref, held, low, at, ref, rows in (
        (far_ref, far_rows, odd, 0, est_ref, send),
        (later_ref, later_rows, odd, 0, band_ref, edge),
        (later_ref, later_rows, odd, edge, dirty_ref, edge),
        (near_ref, near_rows, 1 - odd, 0, est_ref, send),
        (near_ref, near_rows, 1 - odd, send, band_ref, edge),
        (near_ref, near_rows, 1 - odd, send + edge, dirty_ref, edge),
    ):
        start = pl.multiple_of(low * (height - rows), 8)
        k = len(loads)
        piece = (slice(None), slice(at, at + rows))
        loads.append(pltpu.make_async_copy(ref.at[:, pl.ds(start, rows)], held.at[piece], in_sems.at[k]))
        stores.append(pltpu.make_async_copy(held.at[piece], out_ref.at[piece], out_sems.at[k]))
    for load in loads:
        load.start()
    for load, store in zip(loads, stores):
        load.wait()
        store.start()
    for store in stores:
        store.wait()


def banded(line, rows):
    return pltpu.roll(
        jnp.broadcast_to(line, (rows, LANES)), 0, 1, stride=1, stride_axis=0
    )


def square_band(line, width, half):
    around = banded(line, LANES)
    offset = lax.broadcasted_iota(jnp.int32, (LANES, LANES), 1) - lax.broadcasted_iota(
        jnp.int32, (LANES, LANES), 0
    )
    parts = []
    for piece in split(around):
        piece = piece.astype(F32)
        middle = jnp.where(jnp.abs(offset) <= half, piece, 0.0).astype(BF16)
        right = jnp.where(offset <= half - LANES, piece, 0.0).astype(BF16)
        left = jnp.where(offset >= LANES - half, piece, 0.0).astype(BF16)
        blank = jnp.zeros((LANES, LANES), BF16)
        tiles = width // LANES
        kinds = {0: middle, 1: right, -1: left}
        parts.append(
            jnp.concatenate(
                [
                    jnp.concatenate([kinds.get(j - i, blank) for j in range(tiles)], axis=1)
                    for i in range(tiles)
                ],
                axis=0,
            )
        )
    return parts


def matrices_kernel(
    flags_ref, cols_ref, rows_ref, wav_ref, mats_ref, far_band_ref, far_mats_ref, adj_ref, wav_free_ref, wav_touched_ref,
    around_head_ref, around_rest_ref, back_head_ref, back_rest_ref,
    wav_head_ref, wav_rest_ref, wav_head_t_ref, wav_rest_t_ref, lines_ref,
):
    chans, width = around_head_ref.shape[:2]
    send = far_mats_ref.shape[2] // 3
    height, reach = adj_ref.shape[1], adj_ref.shape[2] // 3
    half, touched = height // 2, far_band_ref.shape[0]
    free = reach - touched
    edge = (reach - height) // 2
    facet, facets = lax.axis_index("facet"), lax.axis_size("facet")
    odd = lax.rem(facet, 2) == 1

    def inside(shape, dim):
        at = lax.broadcasted_iota(jnp.int32, shape, dim)
        low = jnp.where(facet > 0, 0, edge)
        high = jnp.where(facet < facets - 1, reach, reach - edge)
        return jnp.where((at >= low) & (at < high), 1.0, 0.0)

    def placed(taps, first, back):
        count = taps.shape[1]
        lane = lax.broadcasted_iota(jnp.int32, (count, LANES), 1)
        tap = lax.broadcasted_iota(jnp.int32, (count, LANES), 0)
        at = jnp.where(lane >= first, lane - first, lane - first + LANES) if first >= 0 else jnp.where(
            lane - first < LANES, lane - first, lane - first - LANES
        )
        pick = jnp.where((count - 1 - at if back else at) == tap, 1.0, 0.0)
        return jnp.dot(taps, pick, precision=lax.Precision.HIGHEST, preferred_element_type=F32)

    def put(at, cols, rows, half_c, half_r):
        lines = jnp.concatenate(
            [
                placed(cols, -half_c, True), placed(cols, -half_c, False),
                placed(rows, edge - half_r, False), placed(rows, edge - half_r, True),
            ],
            axis=1,
        )
        for c in range(lines.shape[0]):
            lines_ref[at + c] = lines[c : c + 1]

    put(0, cols_ref[...], rows_ref[...], PSF_HALF, PSF_HALF)
    put(chans, wav_ref[1:2], wav_ref[0:1], WAV_HALF, WAV_HALF)

    def line(c, k):
        return lines_ref[c, :, k * LANES : (k + 1) * LANES]

    def wide_rows(matrix):
        first, second = split(matrix)
        first, second = first.astype(F32), second.astype(F32)
        return jnp.concatenate([first, first, second], axis=1).astype(BF16)

    wav_head_ref[...], wav_rest_ref[...] = square_band(line(chans, 0), width, WAV_HALF)
    wav_head_t_ref[...], wav_rest_t_ref[...] = square_band(line(chans, 1), width, WAV_HALF)

    def halves(matrix):
        low, high = matrix[:half], matrix[half:]
        return jnp.where(odd, low, high), jnp.where(odd, high, low)

    def reached(matrix):
        return jnp.where(odd, matrix[:free], matrix[touched:]), jnp.where(odd, matrix[free:], matrix[:touched])

    near, far = halves(banded(line(chans, 3), height)[:, :reach])
    wav_free_ref[...] = wide_rows(
        jnp.concatenate([jnp.where(odd, x[:, :free], x[:, touched:]) for x in (near, far)], axis=0)
    )
    wav_touched_ref[...] = wide_rows(jnp.where(odd, far[:, free:], far[:, :touched]))

    def by_side(matrix):
        low, high = matrix[:, :send], matrix[:, send + height : 2 * send + height]
        first, second = matrix[:, send : send + half], matrix[:, send + half : send + height]
        own = jnp.where(odd, first, second), jnp.where(odd, second, first)
        near, far = jnp.where(odd, low, high), jnp.where(odd, high, low)
        return wide_rows(jnp.concatenate([*own, near], axis=1)), wide_rows(far)

    band = banded(line(chans, 2), reach) * inside((reach, LANES), 0)
    band, far_band = by_side(jnp.concatenate(reached(band), axis=0))
    far_band_ref[...] = far_band[free:]

    def body(c, carry):
        head, rest = square_band(line(c, 0), width, PSF_HALF)
        back_head, back_rest = square_band(line(c, 1), width, PSF_HALF)
        back_head_ref[c] = back_head
        back_rest_ref[c] = back_rest
        around = (
            jnp.dot(head, back_head, preferred_element_type=F32)
            + jnp.dot(rest, back_head, preferred_element_type=F32)
            + jnp.dot(head, back_rest, preferred_element_type=F32)
        )
        around_head_ref[c], around_rest_ref[c] = split(around)
        flag = flags_ref[c].astype(F32)
        adjoint = banded(line(c, 3), height) * flag
        adjoint = jnp.concatenate(halves(adjoint), axis=0)
        adj_ref[c] = wide_rows(adjoint[:, :reach])
        adjoint = adjoint * inside((height, LANES), 1)
        forward = banded(line(c, 2), reach)
        first, second = split(adjoint[:, :reach])
        head, rest = split(forward)
        normal = (
            jnp.dot(first, head, preferred_element_type=F32)
            + jnp.dot(second, head, preferred_element_type=F32)
            + jnp.dot(first, rest, preferred_element_type=F32)
        )
        mats_ref[c, :reach] = band
        mats_ref[c, reach:], far = by_side(normal)
        far_mats_ref[c] = far[half:]
        return carry

    lax.fori_loop(0, chans, body, 0, unroll=True)


def first_columns_kernel(odd_ref, own_ref, head_ref, rest_ref, near_ref, far_ref, band_ref, sum_ref):
    chans, height, width = own_ref.shape
    half = height // 2
    odd = odd_ref[0] == 1
    total = jnp.zeros((height, width), F32)
    for c in range(0, chans, GROUP):
        n = min(GROUP, chans - c)
        low, high = own_ref[c : c + n, :half], own_ref[c : c + n, half:]
        near, far = jnp.where(odd, low, high), jnp.where(odd, high, low)
        near_ref[c : c + n] = near
        far_ref[c : c + n] = far
        rows = jnp.concatenate([near, far], axis=1)
        band = times_columns(rows.reshape(n * height, width), head_ref[...], rest_ref[...])
        band = band.reshape(n, height, width)
        band_ref[c : c + n] = band
        total = total + jnp.sum(band * band, axis=0)
    sum_ref[...] = total


def first_gradient_kernel(part_ref, head_ref, rest_ref, grad_ref):
    def body(c, carry):
        grad_ref[c] = times_columns(part_ref[c], head_ref[c], rest_ref[c])
        return carry

    lax.fori_loop(0, part_ref.shape[0], body, 0, unroll=True)


def gradient_kernel(part_ref, halo_ref, far_mats_ref, head_ref, rest_ref, data_ref, _, grad_ref, whole_ref):
    chans, height = part_ref.shape[:2]
    half = height // 2

    def add_far(c, carry):
        far = jnp.dot(far_mats_ref[c], stacked(halo_ref[c]), preferred_element_type=F32)
        whole_ref[c, :half] = part_ref[c, :half]
        whole_ref[c, half:] = part_ref[c, half:] + far
        return carry

    def body(c, carry):
        grad_ref[c] = times_columns(whole_ref[c], head_ref[c], rest_ref[c]) - data_ref[c]
        return carry

    lax.fori_loop(0, chans, add_far, 0, unroll=True)
    lax.fori_loop(0, chans, body, 0, unroll=True)


def scaled(sums_refs, rows, radius):
    total = sums_refs[0][:rows]
    for ref in sums_refs[1:]:
        total = total + ref[:rows]
    length = jnp.sqrt(total)
    return radius / jnp.maximum(length, radius)


def radius_kernel(factor, *refs):
    *sums_refs, out_ref = refs
    skip = sums_refs[0].shape[0] - out_ref.shape[0]
    total = sums_refs[0][skip:]
    for ref in sums_refs[1:]:
        total = total + ref[skip:]
    out_ref[...] = factor / (jnp.sqrt(total) + WEIGHT_OFFSET)


def early_kernel(n_sums, *refs):
    sums_refs, refs = refs[:n_sums], refs[n_sums:]
    (
        radius_ref, moved_u_ref, moved1_ref, near_ref, far_ref, grad_ref, rows_ref, head_ref, rest_ref,
        dual_u_ref, dual1_ref, new_near_ref, half_far_ref,
    ) = refs
    chans, half, width = near_ref.shape
    height, free = 2 * half, moved_u_ref.shape[1]
    scale = scaled(sums_refs, free + height, radius_ref[: free + height])
    scale_u, scale1 = scale[:free], scale[free:]
    for c0 in range(0, chans, GROUP // 2):
        n = min(GROUP // 2, chans - c0)
        dual1 = moved1_ref[c0 : c0 + n] * scale1[None]
        dual1_ref[c0 : c0 + n] = dual1
        across = times_columns(dual1.reshape(n * height, width), head_ref[...], rest_ref[...])
        for c in range(c0, c0 + n):
            dual = moved_u_ref[c] * scale_u
            dual_u_ref[c] = dual
            down = jnp.dot(rows_ref[...], stacked(dual), preferred_element_type=F32)
            at = (c - c0) * height
            step = STEP_PRIMAL * (grad_ref[c] + (down + across[at : at + height]))
            new_near_ref[c] = jnp.maximum(near_ref[c] - step[:half], 0.0)
            half_far_ref[c] = far_ref[c] - step[half:]


def late_kernel(n_sums, odd_ref, *refs):
    sums_refs, refs = refs[:n_sums], refs[n_sums:]
    radius_ref, moved_ref, half_far_ref, rows_ref, dual_ref, new_ref, *rim_refs = refs
    chans, touched = moved_ref.shape[:2]
    odd = odd_ref[0] == 1
    scale = scaled(sums_refs, touched, radius_ref[radius_ref.shape[0] - touched :])

    def body(c, carry):
        dual = moved_ref[c] * scale
        dual_ref[c] = dual
        down = jnp.dot(rows_ref[...], stacked(dual), preferred_element_type=F32)
        new = jnp.maximum(half_far_ref[c] - STEP_PRIMAL * down, 0.0)
        new_ref[c] = new
        for ref in rim_refs:
            rim = ref.shape[1]
            ref[c] = jnp.where(odd, new[new.shape[0] - rim :], new[:rim])
        return carry

    lax.fori_loop(0, chans, body, 0, unroll=True)


def first_update_kernel(
    dual_u_ref, dual_t_ref, dual1_ref, near_ref, far_ref, grad_ref, data_ref, rows_ref, rows_t_ref, head_ref,
    rest_ref, new_near_ref, new_far_ref,
):
    chans, half, width = near_ref.shape
    height = 2 * half
    for c0 in range(0, chans, GROUP // 2):
        n = min(GROUP // 2, chans - c0)
        across = times_columns(
            dual1_ref[c0 : c0 + n].reshape(n * height, width), head_ref[...], rest_ref[...]
        )
        for c in range(c0, c0 + n):
            down = jnp.dot(rows_ref[...], stacked(dual_u_ref[c]), preferred_element_type=F32)
            late = jnp.dot(rows_t_ref[...], stacked(dual_t_ref[c]), preferred_element_type=F32)
            at = (c - c0) * height
            step = (grad_ref[c] - data_ref[c]) + (down + across[at : at + height])
            new_near_ref[c] = jnp.maximum(near_ref[c] - STEP_PRIMAL * step[:half], 0.0)
            new_far_ref[c] = jnp.maximum(far_ref[c] - STEP_PRIMAL * (step[half:] + late), 0.0)


def final_early_kernel(n_sums, odd_ref, *refs):
    sums_refs, refs = refs[:n_sums], refs[n_sums:]
    radius_ref, moved_u_ref, moved1_ref, out_ref, across, down, sems = refs
    chans, height, _ = moved1_ref.shape
    half, free, kept = height // 2, moved_u_ref.shape[1], down.shape[1]
    odd = odd_ref[0] == 1
    scale = scaled(sums_refs, free + height, radius_ref[: free + height])
    start = pl.multiple_of((1 - lax.rem(lax.axis_index("facet"), 2)) * (height - kept), 8)
    low, high = out_ref.at[:, 1], out_ref.at[:, 0, pl.ds(start, kept)]
    for c in range(chans):
        dual = moved1_ref[c] * scale[free:]
        near, far = dual[:half], dual[half:]
        across[c, :half] = jnp.where(odd, near, far)
        across[c, half:] = jnp.where(odd, far, near)
    copies = [pltpu.make_async_copy(across, low, sems.at[0]), pltpu.make_async_copy(down, high, sems.at[1])]
    copies[0].start()
    for c in range(chans):
        dual = moved_u_ref[c] * scale[:free]
        down[c] = jnp.where(odd, dual[free - kept :], dual[:kept])
    copies[1].start()
    for copy in copies:
        copy.wait()


def final_late_kernel(n_sums, odd_ref, *refs):
    sums_refs, refs = refs[:n_sums], refs[n_sums:]
    radius_ref, moved_ref, _, out_ref, down, sem = refs
    chans, height, width = out_ref.shape[0], *out_ref.shape[2:]
    touched, rest = moved_ref.shape[1], down.shape[1]
    odd = odd_ref[0] == 1
    scale = scaled(sums_refs, touched, radius_ref[radius_ref.shape[0] - touched :])
    for c in range(chans):
        dual = moved_ref[c] * scale
        down[c] = jnp.where(odd, dual[:rest], dual[touched - rest :])
    start = pl.multiple_of(lax.rem(lax.axis_index("facet"), 2) * (height - rest), 8)
    copy = pltpu.make_async_copy(down, out_ref.at[:, 0, pl.ds(start, rest)], sem)
    copy.start()
    copy.wait()


def publish_kernel(near_ref, far_ref, _, out_ref, sems):
    half = near_ref.shape[1]
    odd = lax.rem(lax.axis_index("facet"), 2)
    copies = [
        pltpu.make_async_copy(
            ref, out_ref.at[:, pl.ds(pl.multiple_of(low * half, 8), half)], sems.at[k]
        )
        for k, (ref, low) in enumerate(((near_ref, 1 - odd), (far_ref, odd)))
    ]
    for copy in copies:
        copy.start()
    for copy in copies:
        copy.wait()


def trade(values, across):
    n = lax.axis_size("facet")
    if across:
        pairs = [(i, ((i + 1) ^ 1) - 1) for i in range(n) if 0 <= ((i + 1) ^ 1) - 1 < n]
    else:
        pairs = [(i, i ^ 1) for i in range(n)]
    return lax.ppermute(values, "facet", pairs)


def peers(n, low):
    return sorted(range(1, min(4, n // low)), key=lambda k: -k.bit_count())


def gathered(sums):
    n = lax.axis_size("chan")
    if n & (n - 1):
        return [lax.psum(sums, "chan")]
    low = 1
    terms = [sums]
    while low < n:
        total = terms[0]
        for term in terms[1:]:
            total = total + term
        terms = [total]
        for k in peers(n, low):
            terms.append(lax.ppermute(total, "chan", [(i, i ^ (k * low)) for i in range(n)]))
        low *= min(4, n // low)
    return terms


def on_device(
    dirty_image, image_start, dual_start, psf_rows, psf_cols, wavelet_taps, channel_flags
):
    chans, height, width = image_start.shape
    total_chans = chans * lax.axis_size("chan")
    edge = max(PSF_HALF, WAV_HALF)
    reach, send = height + 2 * edge, 2 * edge
    passes = OUTER * INNER
    odd = (lax.axis_index("facet") % 2).astype(jnp.int32)[None]

    half, touched = height // 2, send
    free = reach - touched
    if half != send:
        raise ValueError("facet height")

    def rows(count):
        return (chans, count, width), F32

    own, side, wavy, late_rows = rows(height), rows(half), rows(free), rows(touched)
    late_sum = ((touched, width), F32)
    summed = ((reach + height, width), F32)
    square = ((width, width), BF16)
    squares = ((chans, width, width), BF16)

    inputs = [pltpu.with_memory_space_constraint(x, pltpu.HBM) for x in (image_start, dual_start, dirty_image)]

    in_hbm = pl.BlockSpec(memory_space=pltpu.HBM)
    packs = (rows(send), rows(2 * edge), rows(send + 2 * edge))
    far, later, near = pl.pallas_call(
        pack_kernel,
        out_shape=[jax.ShapeDtypeStruct(*pack) for pack in packs],
        in_specs=[in_hbm] * 3,
        out_specs=[in_hbm] * 3,
        scratch_shapes=[pltpu.VMEM(*pack) for pack in packs] + [pltpu.SemaphoreType.DMA((6,))] * 2,
        compiler_params=PARAMS,
        name="pack",
    )(*inputs)
    far = trade(far, True)
    later = trade(later, True)

    (
        mats, far_band, far_mats, adjoint, wav_free, wav_touched, around_head, around_rest, back_head, back_rest,
        wav_head, wav_rest, wav_head_t, wav_rest_t,
    ) = call(
        matrices_kernel, (channel_flags, psf_cols, psf_rows, wavelet_taps),
        (
            ((chans, reach + height, 3 * (height + send)), BF16), ((touched, 3 * send), BF16),
            ((chans, half, 3 * send), BF16), ((chans, height, 3 * reach), BF16),
            ((height, 3 * free), BF16), ((half, 3 * touched), BF16),
            squares, squares, squares, squares, square, square, square, square,
        ),
        1, scratch=(pltpu.VMEM((chans + 1, 1, 4 * LANES), F32),),
    )
    near = trade(near, False)
    est_near, est_far, band1, sum1 = call(
        first_columns_kernel, (odd, image_start, wav_head, wav_rest),
        (side, side, own, ((height, width), F32)), 1,
    )
    band_u, band_t, part, weight_sums = call(
        first_rows_kernel, (est_near, est_far, near, far, mats, far_band, far_mats, sum1),
        (wavy, late_rows, own, summed),
    )
    grad = call(first_gradient_kernel, (part, around_head, around_rest), (own,))[0]
    dual_u, dual_t, dual1, data = call(
        first_data_kernel, (odd, near, later, dual_start, dirty_image, adjoint, back_head, back_rest),
        (wavy, late_rows, own, own), 1, scratch=(pltpu.VMEM(*own),),
    )
    est_near, est_far = call(
        first_update_kernel,
        (dual_u, dual_t, dual1, est_near, est_far, grad, data, wav_free, wav_touched, wav_head_t, wav_rest_t),
        (side, side),
    )
    rim = est_far
    near = trade(est_near, False)
    for step in range(passes):
        last = step + 1 == passes
        far = trade(rim, True)
        weigh = step % INNER == 0
        moved_u, moved_t, moved1, sums, *bands = call(
            functools.partial(near_kernel, weigh, last),
            (est_near, est_far, near, mats, dual_u, dual_t, band_u, band_t, wav_head, wav_rest, dual1, band1)
            + ((weight_sums,) if weigh else ()),
            (wavy, late_rows, own, ((free + height + (summed[0][0] if weigh else 0), width), F32))
            + (() if last else (wavy, late_rows, own, own)),
        )
        if not last:
            band_u, band_t, part, band1 = bands
        early = gathered(sums)
        if weigh:
            radius = call(functools.partial(radius_kernel, RADIUS_SCALE * total_chans), tuple(early), (summed,))[0]
        moved_t, sums, *bands = call(
            functools.partial(far_kernel, send), (odd, far, far_band, band_t, moved_t),
            (late_rows, late_sum) + (() if last else (late_rows,)), 1,
        )
        if not last:
            band_t = bands[0]
        late = gathered(sums)
        if last:
            image_final = pl.pallas_call(
                publish_kernel,
                out_shape=jax.ShapeDtypeStruct(*own),
                in_specs=[VM, VM, pl.BlockSpec(memory_space=pl.ANY)],
                out_specs=pl.BlockSpec(memory_space=pltpu.HBM),
                scratch_shapes=[pltpu.SemaphoreType.DMA((2,))],
                compiler_params=PARAMS,
                name="publish",
            )(est_near, est_far, sums)
            result = jax.ShapeDtypeStruct((chans, 2, height, width), F32)
            rest = touched - edge
            dual_final = pl.pallas_call(
                functools.partial(final_early_kernel, len(early)),
                out_shape=result,
                in_specs=[SM] + [VM] * (len(early) + 3),
                out_specs=in_hbm,
                scratch_shapes=[
                    pltpu.VMEM(*own), pltpu.VMEM(*rows(height - rest)), pltpu.SemaphoreType.DMA((2,))
                ],
                compiler_params=PARAMS,
                name="final_early",
            )(odd, *early, radius, moved_u, moved1)
            dual_final = pl.pallas_call(
                functools.partial(final_late_kernel, len(late)),
                out_shape=result,
                in_specs=[SM] + [VM] * (len(late) + 2) + [in_hbm],
                out_specs=in_hbm,
                scratch_shapes=[pltpu.VMEM(*rows(rest)), pltpu.SemaphoreType.DMA],
                input_output_aliases={len(late) + 3: 0},
                compiler_params=PARAMS,
                name="final_late",
            )(odd, *late, radius, moved_t, dual_final)
            break
        grad = call(
            gradient_kernel, (part, far, far_mats, around_head, around_rest, data, sums), (own,),
            scratch=(pltpu.VMEM(*own),),
        )[0]
        dual_u, dual1, est_near, half_far = call(
            functools.partial(early_kernel, len(early)),
            (*early, radius, moved_u, moved1, est_near, est_far, grad, wav_free, wav_head_t, wav_rest_t),
            (wavy, own, side, side),
        )
        near = trade(est_near, False)
        if step % INNER == INNER - 1:
            weight_sums = call(squares_kernel, (band_u, band1, band_t), (summed,))[0]
        small = step + 2 == passes
        dual_t, est_far, *rims = call(
            functools.partial(late_kernel, len(late)),
            (odd, *late, radius, moved_t, half_far, wav_touched),
            (late_rows, side) + ((rows(WAV_HALF),) if small else ()), 1,
        )
        rim = rims[0] if small else est_far
    return (image_final, dual_final)


def solution(mesh):
    return jax.shard_map(
        on_device,
        mesh=mesh,
        in_specs=(
            P("chan", "facet", None),
            P("chan", "facet", None),
            P("chan", None, "facet", None),
            P("chan", None),
            P("chan", None),
            P(),
            P("chan"),
        ),
        out_specs=(P("chan", "facet", None), P("chan", None, "facet", None)),
        check_vma=False,
    )
```
